512 devices in a mesh: rcpt: 8 (over x, core), cell: 64 (over z, y).
Axes of the slice: x: 4, y: 4, z: 16, core: 2. Of those that a mesh axis runs over, the one named last changes fastest.
Arguments:
- footprint: bfloat16 [4096, 131072], P(('rcpt', 'cell')), may hold values from -0.015625 to 0.015625
- prior_draws: bfloat16 [128, 131072], P(None, 'cell'), may hold values from -6 to 6
- observed: float32 [4096], P('rcpt'), may hold values from -6 to 6
- obs_noise: float32 [4096, 128], P('rcpt'), may hold values from -6 to 6
- batch_of: int32 [4096], P('rcpt'), may hold values from 0 to 63
- batch_variance: float32 [64], replicated, may hold values from 0.1 to 2
- band_offsets: int32 [3], replicated, may hold values from 1 to 8, as said below
- center_block: float32 [128, 128], replicated, may hold values from -5 to 6.5, as said below
- band_blocks: float32 [3, 128, 128], replicated, may hold values from -1 to 1, as said below
Outputs:
- post_flux: float32 [128, 131072], P('rcpt', 'cell')
- obs_weights: float32 [4096, 128], P(('rcpt', 'cell'))
The draws below stay inside these ranges and needn't reach their ends.
Inputs may be any that keep to these rules, and one draw needn't show every extreme that they name: `band_offsets`: the offsets are distinct, and one of them is 8. `center_block`: symmetric; with band_blocks it makes the prior operator positive definite. `band_blocks`: with center_block it makes the prior operator positive definite.
All inputs are finite; a program needn't handle non-finite values.
Results may differ from the reference program's by a relative error of at most 0.0035.
Values may be sent and summed in bfloat16 or wider, within the bound.
A program may use at most 64 MiB of HBM per device.

```python
import math
import jax
import jax.numpy as jnp
from jax import lax

NC = 131072
NR = 4096
S = 128
KB = 128
NBAND = 3
REACH = 8
NBATCH = 64
ITERS = 2


def draw_band_offsets(key, part):
    lower = (jax.random.permutation(jax.random.fold_in(key, 11), REACH - 1) + 1).astype(jnp.int32)
    others = lower[:NBAND - 1]
    place = jax.random.randint(jax.random.fold_in(key, 12), (), 0, NBAND).astype(jnp.int32)
    slots = jnp.arange(NBAND, dtype=jnp.int32)
    picked = jnp.take(others, jnp.clip(jnp.where(slots < place, slots, slots - 1), 0, NBAND - 2))
    return jnp.where(slots == place, jnp.int32(REACH), picked).astype(jnp.int32)


def draw_center_block(key, part):
    factor = jnp.clip(jax.random.normal(jax.random.fold_in(key, 21), (KB, KB), jnp.float32), -3.0, 3.0)
    square = jnp.dot(factor, factor.T, precision=lax.Precision.HIGHEST) / (2.0 * KB)
    return 1.5 * jnp.eye(KB, dtype=jnp.float32) + 0.5 * (square + square.T)


def draw_band_blocks(key, part):
    source = jnp.clip(jax.random.normal(jax.random.fold_in(key, 31), (NBAND, KB, KB), jnp.float32), -4.0, 4.0)
    return source * (0.1 / math.sqrt(KB))


def set_ends(drawn, own_key, least, high):
    spot = [jax.random.randint(jax.random.fold_in(own_key, axis), (), 0, length) for axis, length in enumerate(drawn.shape)]
    main_axis = drawn.shape.index(max(drawn.shape))
    neighbour = spot[:main_axis] + [(spot[main_axis] + 1) % drawn.shape[main_axis]] + spot[main_axis + 1:]
    return drawn.at[tuple(spot)].set(least).at[tuple(neighbour)].set(high)


def block_scale(own_key, extent, cuts, low, top_value):
    def one(position, blocks):
        draws = jax.random.uniform(jax.random.fold_in(jax.random.fold_in(own_key, 6), position), (blocks,), jnp.float32, low / len(cuts), top_value / len(cuts))
        return jnp.repeat(jnp.exp(draws), extent[position] // blocks).reshape((-1,) + (1,) * (len(extent) - position - 1))

    loudness = one(*cuts[0])
    for cut in cuts[1:]:
        loudness = loudness * one(*cut)
    return loudness


def centred(own_key, dims, deviation, bound, cuts=(), kind=jnp.bfloat16):
    array = jax.random.normal(own_key, dims, jnp.float32) * deviation
    if len(cuts) > 0:
        array = block_scale(own_key, dims, cuts, -0.22, 0.18) * array
    return jnp.clip(array, min=-bound, max=bound).astype(kind)


def setup_inputs(seed: int = 0) -> dict:
    keys = jax.random.split(jax.random.key(seed), 10)
    return {
        "footprint": centred(keys[0], (NR, NC), NC ** -0.5, 0.015625, ((0, 512),)),
        "prior_draws": centred(keys[1], (S, NC), 1.0, 6.0, ((1, 64),)),
        "observed": centred(keys[2], (NR,), 1.0, 6.0, ((0, 8),), jnp.float32),
        "obs_noise": centred(keys[3], (NR, S), 1.0, 6.0, ((0, 8),), jnp.float32),
        "batch_of": set_ends(jax.random.randint(keys[4], (NR,), 0, NBATCH), jax.random.fold_in(keys[4], 1), 0, NBATCH - 1).astype(jnp.int32),
        "batch_variance": jnp.clip(jnp.exp(jax.random.uniform(keys[5], (NBATCH,), jnp.float32, math.log(0.1), math.log(2.0))), 0.1, 2.0),
        "band_offsets": draw_band_offsets(jax.random.fold_in(keys[9], 71), 0),
        "center_block": draw_center_block(jax.random.fold_in(keys[9], 71), 0),
        "band_blocks": draw_band_blocks(jax.random.fold_in(keys[9], 71), 0),
    }


def band_sum(field_in, padded, band_offsets, center_block, band_blocks):
    block_width = center_block.shape[0]
    row_count, cell_parts = field_in.shape
    shaped = (row_count, cell_parts // block_width, block_width)
    running = jnp.einsum('rbk,kj->rbj', field_in.reshape(shaped), center_block, precision=lax.Precision.HIGHEST)
    for band in range(band_blocks.shape[0]):
        offset = band_offsets[band].astype(jnp.int32)
        ahead = lax.dynamic_slice_in_dim(padded, ((REACH + offset) * block_width).astype(jnp.int32), cell_parts, 1)
        behind = lax.dynamic_slice_in_dim(padded, ((REACH - offset) * block_width).astype(jnp.int32), cell_parts, 1)
        running = running + jnp.einsum('rbk,kj->rbj', ahead.reshape(shaped), band_blocks[band], precision=lax.Precision.HIGHEST)
        running = running + jnp.einsum('rbk,jk->rbj', behind.reshape(shaped), band_blocks[band], precision=lax.Precision.HIGHEST)
    return running.reshape(row_count, cell_parts)

def prior_apply(field_in, band_offsets, center_block, band_blocks):
    margin = REACH * center_block.shape[0]
    padded = jnp.pad(field_in, ((0, 0), (margin, margin)))
    return band_sum(field_in, padded, band_offsets, center_block, band_blocks)

def reference(footprint, prior_draws, observed, obs_noise, batch_of, batch_variance, band_offsets, center_block, band_blocks):
    noise_var = batch_variance[batch_of]

    def back_project(vector):
        return jnp.dot(vector.astype(jnp.bfloat16).T, footprint, preferred_element_type=jnp.float32)

    def operate(direction):
        smooth = prior_apply(back_project(direction), band_offsets, center_block, band_blocks).astype(jnp.bfloat16)
        return jnp.dot(footprint, smooth.T, preferred_element_type=jnp.float32) + noise_var[:, None] * direction
    base = jnp.dot(footprint, prior_draws.T, preferred_element_type=jnp.float32)
    residual = observed[:, None] + jnp.sqrt(noise_var)[:, None] * obs_noise - base
    direction = residual
    weights = jnp.zeros_like(residual)
    norm_now = lax.optimization_barrier(jnp.sum(residual * residual, axis=0))
    for iteration in range(ITERS):
        applied = operate(direction)
        step_size = norm_now / lax.optimization_barrier(jnp.sum(direction * applied, axis=0))
        weights = weights + step_size[None, :] * direction
        if iteration + 1 < ITERS:
            residual = residual - step_size[None, :] * applied
            norm_next = lax.optimization_barrier(jnp.sum(residual * residual, axis=0))
            direction = residual + (norm_next / norm_now)[None, :] * direction
            norm_now = norm_next
    posterior = prior_draws.astype(jnp.float32) + prior_apply(back_project(weights), band_offsets, center_block, band_blocks)
    return (posterior, weights)
```

```python
import functools

import jax
import jax.numpy as jnp
from jax import lax
from jax.experimental import pallas as pl
from jax.experimental.pallas import tpu as pltpu
from jax.sharding import PartitionSpec as P

REACH = 8
OWN = 8
LANE = 128
MESH = pl.DeviceIdType.MESH
F32 = jnp.float32
BF16 = jnp.bfloat16


def nt_dot(a, b):
    return lax.dot_general(a, b, (((1,), (1,)), ((), ())), preferred_element_type=F32)


def tn_dot(a, b):
    return lax.dot_general(a, b, (((0,), (0,)), ((), ())), preferred_element_type=F32)


def nn_dot(a, b):
    return lax.dot_general(a, b, (((1,), (0,)), ((), ())), preferred_element_type=F32)


def kernel(
    dims,
    h_ref,
    prior_ref,
    rc_ref,
    nv_ref,
    offsets_ref,
    center_ref,
    bands_ref,
    post_ref,
    weights_ref,
    hbuf,
    hm,
    gath,
    own_prior,
    qp,
    qr,
    vown,
    vb,
    fpart,
    fsend,
    frecv,
    fown,
    fpad,
    smooth,
    sbf,
    resid,
    gvec,
    gplane,
    gsum,
    gz,
    h_sem,
    q_sem,
    v_sem,
    ring_sem,
    f_sem,
    s_sem,
    gp_sem,
    gz_sem,
    loc_sem,
):
    n_r, n_z, n_y, bpp, samples = dims
    n_plane = n_r * n_y
    n_cell = n_z * n_y
    n_half = REACH // bpp
    n_blocks = n_r * bpp
    s_rows = samples // n_r
    hb = bpp // 2
    rows = n_plane * OWN
    xc = lax.axis_index("rcpt")
    cell = lax.axis_index("cell")
    z = lax.div(cell, n_y)
    y = lax.rem(cell, n_y)
    me = xc * n_y + y

    def plane_dev(k):
        p = lax.rem(me + k, n_plane)
        return p, lax.div(p, n_y), lax.rem(p, n_y)

    def z_dev(k):
        zz = lax.rem(z + k + n_z, n_z)
        return zz, (xc, zz * n_y + y)

    def remote(src, dst, send, recv, dev):
        return pltpu.make_async_remote_copy(
            src_ref=src, dst_ref=dst, send_sem=send, recv_sem=recv, device_id=dev, device_id_type=MESH
        )

    def wait_bytes(ref, sem):
        pltpu.make_async_copy(ref, ref, sem).wait()

    local_h = pltpu.make_async_copy(h_ref.at[:, y, xc], hbuf.at[:, me], loc_sem.at[0])
    local_h.start()
    local_p = pltpu.make_async_copy(
        prior_ref.at[pl.ds(pl.multiple_of(xc * s_rows, s_rows), s_rows), :], own_prior, loc_sem.at[1]
    )
    local_p.start()
    pieces = []
    for b in range(bpp):
        column = pl.multiple_of((xc * bpp + b) * LANE, LANE)
        piece = pltpu.make_async_copy(
            prior_ref.at[:, pl.ds(column, LANE)], gath.at[0, z, b], loc_sem.at[2 + b]
        )
        piece.start()
        pieces.append(piece)

    barrier = pltpu.get_barrier_semaphore()

    def greet_plane(k, c):
        _, xx, yy = plane_dev(k)
        pl.semaphore_signal(barrier, inc=1, device_id=(xx, z * n_y + yy), device_id_type=MESH)
        return c

    lax.fori_loop(1, n_plane, greet_plane, 0)

    def greet_z(k, c):
        _, dev = z_dev(k)
        pl.semaphore_signal(barrier, inc=1, device_id=dev, device_id_type=MESH)
        return c

    lax.fori_loop(1, n_z, greet_z, 0)
    edge_lo = (y == 0) & (z > 0)
    edge_hi = (y == n_y - 1) & (z < n_z - 1)

    @pl.when(edge_lo)
    def _():
        def greet(k, c):
            pl.semaphore_signal(barrier, inc=1, device_id=(k, cell - 1), device_id_type=MESH)
            return c

        lax.fori_loop(0, n_r, greet, 0)

    @pl.when(edge_hi)
    def _():
        def greet(k, c):
            pl.semaphore_signal(barrier, inc=1, device_id=(k, cell + 1), device_id_type=MESH)
            return c

        lax.fori_loop(0, n_r, greet, 0)

    greeted = n_plane - 1 + n_z - 1

    @pl.when(edge_lo | edge_hi)
    def _():
        pl.semaphore_wait(barrier, greeted + n_r)

    @pl.when(jnp.logical_not(edge_lo | edge_hi))
    def _():
        pl.semaphore_wait(barrier, greeted)

    def send_h(k, c):
        _, xx, yy = plane_dev(k)
        remote(
            h_ref.at[:, yy, xx], hbuf.at[:, me], h_sem.at[0], h_sem.at[1], (xx, z * n_y + yy)
        ).start()
        return c

    lax.fori_loop(1, n_plane, send_h, 0)
    for piece in pieces:
        piece.wait()

    chains = (
        (0, 1, n_z // 2),
        (0, -1, n_z - 1 - n_z // 2),
        (1, 1, n_z - 1 - n_z // 2),
        (1, -1, n_z // 2),
    )
    short = n_z - 1 - n_z // 2

    def ring(step_fn):
        for ci, chain in enumerate(chains):
            if chain[2] > 0:
                step_fn(ci, chain, 0, True)

        def body(s, c):
            for ci, chain in enumerate(chains):
                step_fn(ci, chain, s, False)
            return c

        lax.fori_loop(1, short, body, 0)
        for s in range(max(short, 1), n_z // 2):
            for ci, chain in enumerate(chains):
                if s < chain[2]:
                    step_fn(ci, chain, s, False)

    def gather_ring(call):
        def copy(ci, chain, s):
            half, sign, _ = chain
            origin = lax.rem(z - sign * s + n_z, n_z)
            _, dev = z_dev(sign)
            part = gath.at[call, origin, pl.ds(half * hb, hb)]
            return remote(part, part, ring_sem.at[call, 0, ci, s], ring_sem.at[call, 1, ci, s], dev)

        def step(ci, chain, s, first):
            if not first:
                copy(ci, chain, s - 1).wait_recv()
            copy(ci, chain, s).start()

        ring(step)
        for ci, chain in enumerate(chains):
            if chain[2] > 0:
                copy(ci, chain, chain[2] - 1).wait_recv()

        def drain(s, c):
            for ci, chain in enumerate(chains):
                copy(ci, chain, s).wait_send()
            return c

        lax.fori_loop(0, short, drain, 0)
        for s in range(short, n_z // 2):
            for ci, chain in enumerate(chains):
                if s < chain[2]:
                    copy(ci, chain, s).wait_send()

    def reduce_ring(call):
        def copy(ci, chain, s):
            _, dev = z_dev(chain[1])
            return remote(
                fsend.at[call, ci, s],
                frecv.at[call, ci, s],
                ring_sem.at[2 + call, 0, ci, s],
                ring_sem.at[2 + call, 1, ci, s],
                dev,
            )

        def step(ci, chain, s, first):
            half, sign, steps = chain
            target = lax.rem(z + sign * (steps - s) + n_z, n_z)
            value = fpart[target, pl.ds(half * hb, hb)]
            if not first:
                copy(ci, chain, s - 1).wait_recv()
                value = value + frecv[call, ci, s - 1].astype(F32)
            fsend[call, ci, s] = value.astype(BF16)
            copy(ci, chain, s).start()

        ring(step)
        for ci, chain in enumerate(chains):
            if chain[2] > 0:
                copy(ci, chain, chain[2] - 1).wait_recv()
        for half in range(2):
            total = fpart[z, pl.ds(half * hb, hb)]
            for ci, chain in enumerate(chains):
                if chain[0] == half and chain[2] > 0:
                    total = total + frecv[call, ci, chain[2] - 1].astype(F32)
            fown[call, pl.ds(half * hb, hb)] = total.astype(BF16)

        def drain(s, c):
            for ci, chain in enumerate(chains):
                copy(ci, chain, s).wait_send()
            return c

        lax.fori_loop(0, short, drain, 0)
        for s in range(short, n_z // 2):
            for ci, chain in enumerate(chains):
                if s < chain[2]:
                    copy(ci, chain, s).wait_send()

    def forward_sum(call):
        def body(k, acc):
            hz = hm[k]
            for b in range(bpp):
                acc = acc + nt_dot(hz[:, b * LANE : (b + 1) * LANE], gath[call, k, b])
            return acc

        acc = lax.fori_loop(0, n_z, body, jnp.zeros((rows, samples), F32))
        qp[call] = acc.reshape(n_plane, OWN, samples)

        def send(k, c):
            p, xx, yy = plane_dev(k)
            remote(
                qp.at[call, p], qr.at[call, me], q_sem.at[call, 0], q_sem.at[call, 1], (xx, z * n_y + yy)
            ).start()
            return c

        lax.fori_loop(1, n_plane, send, 0)
        qr[call, me] = qp[call, me]
        wait_bytes(qr.at[call, pl.ds(0, n_plane - 1)], q_sem.at[call, 1])
        total = jnp.sum(qr[call], axis=0)
        wait_bytes(qp.at[call, pl.ds(0, n_plane - 1)], q_sem.at[call, 0])
        return total

    def share_start(call, value):
        vown[call] = value.astype(BF16)
        vb[call, me] = value.astype(BF16)

        def send(k, c):
            _, xx, yy = plane_dev(k)
            remote(
                vown.at[call], vb.at[call, me], v_sem.at[call, 0], v_sem.at[call, 1], (xx, z * n_y + yy)
            ).start()
            return c

        lax.fori_loop(1, n_plane, send, 0)

    def back(call):
        wait_bytes(vb.at[call, pl.ds(0, n_plane - 1)], v_sem.at[call, 1])
        vector = vb[call].astype(F32).reshape(rows, samples).astype(BF16)

        def body(k, c):
            product = tn_dot(vector, hm[k])
            for b in range(bpp):
                fpart[k, b] = product[:, b * LANE : (b + 1) * LANE]
            return c

        lax.fori_loop(0, n_z, body, 0)
        wait_bytes(vb.at[call, pl.ds(0, n_plane - 1)], v_sem.at[call, 0])

    def spread_field(call):
        @pl.when(cell == 0)
        def _():
            fpad[call, pl.ds(0, REACH)] = jnp.zeros((REACH, s_rows, LANE), BF16)

        @pl.when(cell == n_cell - 1)
        def _():
            fpad[call, pl.ds(REACH + n_blocks, REACH)] = jnp.zeros((REACH, s_rows, LANE), BF16)

        def part(r):
            return fown.at[call, :, pl.ds(pl.multiple_of(r * s_rows, s_rows), s_rows)]

        def send(k, c):
            r = lax.rem(xc + k, n_r)
            remote(
                part(r),
                fpad.at[call, pl.ds(REACH + xc * bpp, bpp)],
                f_sem.at[call, 0],
                f_sem.at[call, 1],
                (r, cell),
            ).start()
            return c

        lax.fori_loop(1, n_r, send, 0)
        low = xc < n_half

        @pl.when(low & (cell > 0))
        def _():
            def send_low(k, c):
                r = lax.rem(xc + k, n_r)
                remote(
                    part(r),
                    fpad.at[call, pl.ds(REACH + n_blocks + xc * bpp, bpp)],
                    f_sem.at[call, 2],
                    f_sem.at[call, 3],
                    (r, cell - 1),
                ).start()
                return c

            lax.fori_loop(0, n_r, send_low, 0)

        @pl.when((xc >= n_r - n_half) & (cell < n_cell - 1))
        def _():
            def send_high(k, c):
                r = lax.rem(xc + k, n_r)
                remote(
                    part(r),
                    fpad.at[call, pl.ds((xc - (n_r - n_half)) * bpp, bpp)],
                    f_sem.at[call, 4],
                    f_sem.at[call, 5],
                    (r, cell + 1),
                ).start()
                return c

            lax.fori_loop(0, n_r, send_high, 0)

        own = pltpu.make_async_copy(
            part(xc), fpad.at[call, pl.ds(REACH + xc * bpp, bpp)], loc_sem.at[2 + bpp + call]
        )
        own.start()
        own.wait()
        body = fpad.at[call, pl.ds(0, (n_r - 1) * bpp)]
        halo = fpad.at[call, pl.ds(0, REACH)]
        wide = fpad.at[call, pl.ds(0, n_blocks)]
        wait_bytes(body, f_sem.at[call, 1])

        @pl.when(cell < n_cell - 1)
        def _():
            wait_bytes(halo, f_sem.at[call, 3])

        @pl.when(cell > 0)
        def _():
            wait_bytes(halo, f_sem.at[call, 5])

        wait_bytes(body, f_sem.at[call, 0])

        @pl.when(low & (cell > 0))
        def _():
            wait_bytes(wide, f_sem.at[call, 2])

        @pl.when((xc >= n_r - n_half) & (cell < n_cell - 1))
        def _():
            wait_bytes(wide, f_sem.at[call, 4])

    def split(matrix):
        high = matrix.astype(BF16)
        return high, (matrix - high.astype(F32)).astype(BF16)

    def prior_apply(call):
        flat = (n_blocks * s_rows, LANE)
        high, low = split(center_ref[...])
        here = fpad[call, pl.ds(REACH, n_blocks)].reshape(flat)
        acc = nn_dot(here, high) + nn_dot(here, low)
        for band in range(bands_ref.shape[0]):
            offset = offsets_ref[band]
            high, low = split(bands_ref[band])
            ahead = fpad[call, pl.ds(REACH + offset, n_blocks)].reshape(flat)
            acc = acc + nn_dot(ahead, high) + nn_dot(ahead, low)
            behind = fpad[call, pl.ds(REACH - offset, n_blocks)].reshape(flat)
            acc = acc + nt_dot(behind, high) + nt_dot(behind, low)
        smooth[call] = acc.reshape(n_blocks, s_rows, LANE)

    row_id = lax.broadcasted_iota(jnp.int32, (s_rows, samples), 0)
    lane_id = lax.broadcasted_iota(jnp.int32, (s_rows, samples), 1)
    own_lane = lane_id == row_id + xc * s_rows

    def to_lanes(column):
        return jnp.sum(jnp.where(own_lane, column, 0.0), axis=0, keepdims=True)

    def to_column(lanes):
        return jnp.sum(jnp.where(own_lane, lanes, 0.0), axis=1, keepdims=True)

    def field_dot(field, image):
        return to_lanes(jnp.sum(jnp.sum(field * image, axis=0), axis=1, keepdims=True))

    def row_dot(a, b):
        return jnp.sum(a * b, axis=0, keepdims=True)

    def total_start(call, first, second):
        gvec[call] = jnp.concatenate(
            [first, second, jnp.zeros((OWN - 2, samples), F32)], axis=0
        )

        def send(k, c):
            _, xx, yy = plane_dev(k)
            remote(
                gvec.at[call],
                gplane.at[call, me],
                gp_sem.at[call, 0],
                gp_sem.at[call, 1],
                (xx, z * n_y + yy),
            ).start()
            return c

        lax.fori_loop(1, n_plane, send, 0)
        gplane[call, me] = gvec[call]

    def total_middle(call):
        wait_bytes(gplane.at[call, pl.ds(0, n_plane - 1)], gp_sem.at[call, 1])
        gsum[call] = jnp.sum(gplane[call], axis=0)

        def send(k, c):
            _, dev = z_dev(k)
            remote(
                gsum.at[call], gz.at[call, z], gz_sem.at[call, 0], gz_sem.at[call, 1], dev
            ).start()
            return c

        lax.fori_loop(1, n_z, send, 0)
        gz[call, z] = gsum[call]
        wait_bytes(gplane.at[call, pl.ds(0, n_plane - 1)], gp_sem.at[call, 0])

    def total_end(call):
        wait_bytes(gz.at[call, pl.ds(0, n_z - 1)], gz_sem.at[call, 1])
        total = jnp.sum(gz[call], axis=0)
        wait_bytes(gz.at[call, pl.ds(0, n_z - 1)], gz_sem.at[call, 0])
        return total[0:1], total[1:2]

    gather_ring(0)
    local_h.wait()
    wait_bytes(hbuf.at[:, pl.ds(0, n_plane - 1)], h_sem.at[1])

    def relayout(k, c):
        hm[k] = hbuf[k].astype(F32).reshape(rows, bpp * LANE).astype(BF16)
        return c

    lax.fori_loop(0, n_z, relayout, 0)

    first = rc_ref[...] - forward_sum(0)
    resid[0] = first
    share_start(0, first)
    back(0)
    reduce_ring(0)
    spread_field(0)
    prior_apply(0)

    sbf[...] = smooth[0].astype(BF16)

    def smooth_dst():
        return gath.at[1, z, :, pl.ds(pl.multiple_of(xc * s_rows, s_rows), s_rows)]

    def send_smooth(k, c):
        r = lax.rem(xc + k, n_r)
        remote(
            sbf.at[pl.ds(r * bpp, bpp)], smooth_dst(), s_sem.at[0], s_sem.at[1], (r, cell)
        ).start()
        return c

    lax.fori_loop(1, n_r, send_smooth, 0)
    keep = pltpu.make_async_copy(sbf.at[pl.ds(xc * bpp, bpp)], smooth_dst(), loc_sem.at[4 + bpp])
    keep.start()
    r0 = resid[0]
    energy = field_dot(fpad[0, pl.ds(REACH, n_blocks)].astype(F32), smooth[0])
    total_start(0, row_dot(r0, r0), energy + row_dot(r0 * nv_ref[...], r0))
    keep.wait()
    others = sbf.at[pl.ds(0, (n_r - 1) * bpp)]
    wait_bytes(others, s_sem.at[1])
    gather_ring(1)
    total_middle(0)
    applied = forward_sum(1) + nv_ref[...] * resid[0]
    wait_bytes(others, s_sem.at[0])
    norm0, curve0 = total_end(0)
    alpha0 = norm0 / curve0
    second = resid[0] - alpha0 * applied
    resid[1] = second
    share_start(1, second)
    total_start(1, row_dot(second, second), jnp.zeros((1, samples), F32))
    back(1)
    total_middle(1)
    reduce_ring(1)
    spread_field(1)
    prior_apply(1)
    norm1, _ = total_end(1)
    beta = norm1 / norm0
    direction = resid[1] + beta * resid[0]
    beta_column = to_column(beta)
    field0 = fpad[0, pl.ds(REACH, n_blocks)].astype(F32)
    field1 = fpad[1, pl.ds(REACH, n_blocks)].astype(F32)
    energy = field_dot(field1 + beta_column * field0, smooth[1] + beta_column * smooth[0])
    total_start(2, energy + row_dot(direction * nv_ref[...], direction), jnp.zeros((1, samples), F32))
    total_middle(2)
    local_p.wait()
    curve1, _ = total_end(2)
    alpha1 = norm1 / curve1
    weights_ref[...] = alpha0 * resid[0] + alpha1 * direction
    scale0 = to_column(alpha0 + alpha1 * beta)
    scale1 = to_column(alpha1)
    for b in range(n_blocks):
        columns = slice(b * LANE, (b + 1) * LANE)
        post_ref[:, columns] = (
            own_prior[:, columns].astype(F32) + scale0 * smooth[0, b] + scale1 * smooth[1, b]
        )
    wait_bytes(hbuf.at[:, pl.ds(0, n_plane - 1)], h_sem.at[0])


def local(
    n_r,
    n_z,
    n_y,
    footprint,
    prior_draws,
    observed,
    obs_noise,
    batch_of,
    batch_variance,
    band_offsets,
    center_block,
    band_blocks,
):
    samples = obs_noise.shape[1]
    n_blocks = prior_draws.shape[1] // LANE
    bpp = n_blocks // n_r
    n_plane = n_r * n_y
    s_rows = samples // n_r
    width = bpp * LANE
    rows = n_plane * OWN
    hb = bpp // 2
    steps = n_z // 2
    start = lax.axis_index("cell") * OWN
    levels = jnp.arange(batch_variance.shape[0], dtype=jnp.int32)
    own_batch = lax.dynamic_slice_in_dim(batch_of, start, OWN, 0)
    own_observed = lax.dynamic_slice_in_dim(observed, start, OWN, 0)
    own_noise = lax.dynamic_slice_in_dim(obs_noise, start, OWN, 0)
    matches = (own_batch[:, None] == levels[None, :]).astype(F32)
    noise_var = jnp.sum(matches * batch_variance[None, :], axis=1)
    target = own_observed[:, None] + jnp.sqrt(noise_var)[:, None] * own_noise
    noise_wide = jnp.broadcast_to(noise_var[:, None], (OWN, samples))
    tiles = footprint.reshape(OWN, n_z, n_y, n_r, width).transpose(1, 2, 3, 0, 4)
    vmem = pl.BlockSpec(memory_space=pltpu.VMEM)
    hbm = pl.BlockSpec(memory_space=pl.ANY)
    dma = pltpu.SemaphoreType.DMA
    return pl.pallas_call(
        functools.partial(kernel, (n_r, n_z, n_y, bpp, samples)),
        out_shape=(
            jax.ShapeDtypeStruct((s_rows, n_blocks * LANE), F32),
            jax.ShapeDtypeStruct((OWN, samples), F32),
        ),
        in_specs=[hbm, hbm, vmem, vmem, pl.BlockSpec(memory_space=pltpu.SMEM), vmem, vmem],
        out_specs=(vmem, vmem),
        scratch_shapes=[
            pltpu.VMEM((n_z, n_plane, OWN, width), BF16),
            pltpu.VMEM((n_z, rows, width), BF16),
            pltpu.VMEM((2, n_z, bpp, samples, LANE), BF16),
            pltpu.VMEM((s_rows, n_blocks * LANE), BF16),
            pltpu.VMEM((2, n_plane, OWN, samples), F32),
            pltpu.VMEM((2, n_plane, OWN, samples), F32),
            pltpu.VMEM((2, OWN, samples), BF16),
            pltpu.VMEM((2, n_plane, OWN, samples), BF16),
            pltpu.VMEM((n_z, bpp, samples, LANE), F32),
            pltpu.VMEM((2, 4, steps, hb, samples, LANE), BF16),
            pltpu.VMEM((2, 4, steps, hb, samples, LANE), BF16),
            pltpu.VMEM((2, bpp, samples, LANE), BF16),
            pltpu.VMEM((2, n_blocks + 2 * REACH, s_rows, LANE), BF16),
            pltpu.VMEM((2, n_blocks, s_rows, LANE), F32),
            pltpu.VMEM((n_blocks, s_rows, LANE), BF16),
            pltpu.VMEM((2, OWN, samples), F32),
            pltpu.VMEM((3, OWN, samples), F32),
            pltpu.VMEM((3, n_plane, OWN, samples), F32),
            pltpu.VMEM((3, OWN, samples), F32),
            pltpu.VMEM((3, n_z, OWN, samples), F32),
            dma((2,)),
            dma((2, 2)),
            dma((2, 2)),
            dma((4, 2, 4, steps)),
            dma((2, 6)),
            dma((2,)),
            dma((3, 2)),
            dma((3, 2)),
            dma((5 + bpp,)),
        ],
        compiler_params=pltpu.CompilerParams(
            collective_id=0, has_side_effects=True, vmem_limit_bytes=56 * 1024 * 1024
        ),
    )(tiles, prior_draws, target, noise_wide, band_offsets, center_block, band_blocks)


def solution(mesh, n_y=4):
    n_r = mesh.shape["rcpt"]
    n_z = mesh.shape["cell"] // n_y
    return jax.shard_map(
        functools.partial(local, n_r, n_z, n_y),
        mesh=mesh,
        in_specs=(
            P(("rcpt", "cell"), None),
            P(None, "cell"),
            P("rcpt"),
            P("rcpt", None),
            P("rcpt"),
            P(),
            P(),
            P(),
            P(),
        ),
        out_specs=(P("rcpt", "cell"), P(("rcpt", "cell"), None)),
        check_vma=False,
    )
```

```python
import functools

import jax
import jax.numpy as jnp
from jax import lax
from jax.experimental import pallas as pl
from jax.experimental.pallas import tpu as pltpu
from jax.sharding import PartitionSpec as P

REACH = 8
SPLIT = 1
LOW = 2
STRIDE = 13
OWN = 8
LANE = 128
MESH = pl.DeviceIdType.MESH
F32 = jnp.float32
BF16 = jnp.bfloat16


def nt_dot(a, b):
    return lax.dot_general(a, b, (((1,), (1,)), ((), ())), preferred_element_type=F32)


def tn_dot(a, b):
    return lax.dot_general(a, b, (((0,), (0,)), ((), ())), preferred_element_type=F32)


def nn_dot(a, b):
    return lax.dot_general(a, b, (((1,), (0,)), ((), ())), preferred_element_type=F32)


def kernel(
    dims,
    h_ref,
    prior_ref,
    observed_hbm,
    noise_hbm,
    batch_hbm,
    variance_hbm,
    offsets_ref,
    center_hbm,
    bands_hbm,
    post_ref,
    weights_ref,
    hbuf,
    hm,
    gath,
    own_prior,
    qp,
    qr,
    vown,
    vb,
    fpart,
    fsend,
    frecv,
    fown,
    fpad,
    smooth,
    sbf,
    resid,
    gvec,
    gplane,
    gsum,
    gz,
    qacc,
    observed_ref,
    noise_ref,
    batch_ref,
    variance_ref,
    center_ref,
    bands_ref,
    h_sem,
    q_sem,
    v_sem,
    ring_sem,
    f_sem,
    s_sem,
    gp_sem,
    gz_sem,
    loc_sem,
):
    n_r, n_z, n_y, n_low, bpp, samples = dims
    n_plane = n_r * n_y * n_low
    n_cell = n_z * n_low * n_y
    n_half = REACH // bpp
    n_blocks = n_r * bpp
    s_rows = samples // n_r
    hb = bpp // 2
    rows = n_plane * OWN
    xc = lax.axis_index("rcpt")
    cell = lax.axis_index("cell")
    near = n_y * n_low
    z = lax.div(cell, near)
    within = lax.rem(cell, near)
    me = xc * near + within

    def plane_dev(i):
        p = lax.rem(me + i * STRIDE, n_plane)
        xx, low = lax.div(p, near), lax.rem(p, near)
        return p, xx, low, (xx, z * near + low)

    def z_dev(k):
        zz = lax.rem(z + k + n_z, n_z)
        return zz, (xc, zz * near + within)

    def remote(src, dst, send, recv, dev):
        return pltpu.make_async_remote_copy(
            src_ref=src, dst_ref=dst, send_sem=send, recv_sem=recv, device_id=dev, device_id_type=MESH
        )

    def wait_bytes(ref, sem):
        pltpu.make_async_copy(ref, ref, sem).wait()

    local_h = pltpu.make_async_copy(h_ref.at[:, within, xc], hbuf.at[:, me], loc_sem.at[0])
    local_p = pltpu.make_async_copy(
        prior_ref.at[pl.ds(pl.multiple_of(xc * s_rows, s_rows), s_rows), :], own_prior, loc_sem.at[1]
    )
    pieces = []
    for b in range(bpp):
        column = pl.multiple_of((xc * bpp + b) * LANE, LANE)
        piece = pltpu.make_async_copy(
            prior_ref.at[:, pl.ds(column, LANE)], gath.at[0, z, b], loc_sem.at[2 + b]
        )
        piece.start()
        pieces.append(piece)

    barrier = pltpu.get_barrier_semaphore()

    def greet_plane(k, c):
        pl.semaphore_signal(barrier, inc=1, device_id=plane_dev(k)[3], device_id_type=MESH)
        return c

    lax.fori_loop(1, n_plane, greet_plane, 0)

    for sign in (1, -1):
        pl.semaphore_signal(barrier, inc=1, device_id=z_dev(sign)[1], device_id_type=MESH)
    edge_lo = (within == 0) & (z > 0)
    edge_hi = (within == near - 1) & (z < n_z - 1)

    @pl.when(edge_lo)
    def _():
        def greet(k, c):
            pl.semaphore_signal(barrier, inc=1, device_id=(k, cell - 1), device_id_type=MESH)
            return c

        lax.fori_loop(0, n_r, greet, 0)

    @pl.when(edge_hi)
    def _():
        def greet(k, c):
            pl.semaphore_signal(barrier, inc=1, device_id=(k, cell + 1), device_id_type=MESH)
            return c

        lax.fori_loop(0, n_r, greet, 0)

    greeted = n_plane - 1 + 2

    @pl.when(edge_lo | edge_hi)
    def _():
        pl.semaphore_wait(barrier, greeted + n_r)

    @pl.when(jnp.logical_not(edge_lo | edge_hi))
    def _():
        pl.semaphore_wait(barrier, greeted)

    flat = n_r * n_y
    level = lax.div(within, n_y)
    mine = xc * n_y + lax.rem(within, n_y)

    def send_h(i, hop):
        t = lax.rem(mine + i * STRIDE, flat)
        xx = lax.div(t, n_y)
        low = lax.rem(level + hop, n_low) * n_y + lax.rem(t, n_y)
        remote(
            h_ref.at[:, low, xx], hbuf.at[:, me], h_sem.at[0], h_sem.at[1], (xx, z * near + low)
        ).start()

    def send_same(i, c):
        send_h(i, 0)
        return c

    lax.fori_loop(1, flat, send_same, 0)
    batch = flat * (n_low - 1) // (n_z // 2)

    def send_batch(s):
        def body(i, c):
            send_h(lax.rem(i, flat), 1 + lax.div(i, flat))
            return c

        lax.fori_loop(s * batch, (s + 1) * batch, body, 0)

    local_h.start()
    local_p.start()
    loads = [
        pltpu.make_async_copy(src, dst, loc_sem.at[5 + bpp + i])
        for i, (src, dst) in enumerate(
            (
                (observed_hbm, observed_ref),
                (noise_hbm.at[pl.ds(pl.multiple_of(cell * OWN, OWN), OWN), :], noise_ref),
                (batch_hbm, batch_ref),
                (variance_hbm, variance_ref),
                (center_hbm, center_ref),
                (bands_hbm, bands_ref),
            )
        )
    ]
    for load in loads:
        load.start()
    for piece in pieces:
        piece.wait()

    steps = n_z // 2
    short = n_z - 1 - steps
    middle = max(1, short // 2 + 1)
    sub = samples // SPLIT
    chains = []
    for part in range(SPLIT):
        for half, sign, count in ((0, 1, steps), (0, -1, short), (1, 1, short), (1, -1, steps)):
            chains.append((half, part, sign, count))

    def rotate(k):
        return lax.rem(z + k + n_z, n_z)

    def ring(step_fn, after_step, hook_first, hook_middle):
        for ci, chain in enumerate(chains):
            if chain[3] > 0:
                step_fn(ci, chain, 0, True)
        after_step(0)
        hook_first()

        def body(s, c):
            for ci, chain in enumerate(chains):
                step_fn(ci, chain, s, False)
            after_step(s)
            return c

        lax.fori_loop(1, middle, body, 0)
        hook_middle()
        lax.fori_loop(middle, short, body, 0)
        for s in range(max(short, 1), steps):
            for ci, chain in enumerate(chains):
                if s < chain[3]:
                    step_fn(ci, chain, s, False)
                else:
                    step_fn(ci, chain, s, None)
            after_step(s)

    def drain(copy):
        def body(s, c):
            for ci, chain in enumerate(chains):
                copy(ci, chain, s).wait_send()
            return c

        lax.fori_loop(0, short, body, 0)
        for s in range(short, steps):
            for ci, chain in enumerate(chains):
                if s < chain[3]:
                    copy(ci, chain, s).wait_send()

    def gather_copy(call, ci, chain, s):
        half, part, sign, _ = chain
        origin = rotate(-sign * s)
        piece = gath.at[
            call, origin, pl.ds(half * hb, hb), pl.ds(part * sub, sub)
        ]
        return remote(
            piece, piece, ring_sem.at[call, 0, ci, s], ring_sem.at[call, 1, ci, s], z_dev(sign)[1]
        )

    def accumulate(call, k):
        hz = hm[k]
        for b in range(bpp):
            qacc[...] += nt_dot(hz[:, b * LANE : (b + 1) * LANE], gath[call, k, b])

    def gather_ring(call, multiply, hook_first, hook_middle):
        copy = functools.partial(gather_copy, call)

        def step(ci, chain, s, first):
            if first is not True:
                if s - 1 < chain[3] if isinstance(s, int) else True:
                    copy(ci, chain, s - 1).wait_recv()
            if first is not None:
                copy(ci, chain, s).start()

        def after_step(s):
            if not multiply:
                send_batch(s)
                return
            if isinstance(s, int) and s == 0:
                qacc[...] = jnp.zeros((rows, samples), F32)
                accumulate(call, z)
                return
            accumulate(call, rotate(-s))
            accumulate(call, rotate(s))

        ring(step, after_step, hook_first, hook_middle)
        for ci, chain in enumerate(chains):
            if chain[3] == steps:
                copy(ci, chain, steps - 1).wait_recv()
            elif chain[3] == 0:
                pass
        if multiply:
            accumulate(call, rotate(steps))

    def reduce_copy(call, ci, chain, s):
        return remote(
            fsend.at[call, ci, s],
            frecv.at[call, ci, s],
            ring_sem.at[2 + call, 0, ci, s],
            ring_sem.at[2 + call, 1, ci, s],
            z_dev(chain[2])[1],
        )

    def reduce_ring(call, hook_first, hook_middle):
        copy = functools.partial(reduce_copy, call)
        wait_bytes(vb.at[call, pl.ds(0, n_plane - 1)], v_sem.at[call, 1])
        vector = vb[call].astype(F32).reshape(rows, samples).astype(BF16)

        def project(k):
            product = tn_dot(vector, hm[k])
            for b in range(bpp):
                fpart[k, b] = product[:, b * LANE : (b + 1) * LANE]

        for k in sorted({rotation % n_z for rotation in (steps, steps - 1, 1 - steps)}):
            project(rotate(k))

        def step(ci, chain, s, first):
            half, part, sign, count = chain
            if first is None:
                return
            target = rotate(sign * (count - s))
            value = fpart[target, pl.ds(half * hb, hb), pl.ds(part * sub, sub)]
            if first is not True:
                copy(ci, chain, s - 1).wait_recv()
                value = value + frecv[call, ci, s - 1].astype(F32)
            fsend[call, ci, s] = value.astype(BF16)
            copy(ci, chain, s).start()

        def after_step(s):
            if isinstance(s, int) and steps - 2 - s < 0:
                return
            if isinstance(s, int) and steps - 2 - s == 0:
                project(z)
                return
            project(rotate(steps - 2 - s))
            project(rotate(s + 2 - steps))

        ring(step, after_step, hook_first, hook_middle)
        for ci, chain in enumerate(chains):
            if chain[3] > 0:
                copy(ci, chain, chain[3] - 1).wait_recv()
        for half in range(2):
            for part in range(SPLIT):
                where = (z, pl.ds(half * hb, hb), pl.ds(part * sub, sub))
                total = fpart[where]
                for ci, chain in enumerate(chains):
                    if chain[:2] == (half, part) and chain[3] > 0:
                        total = total + frecv[call, ci, chain[3] - 1].astype(F32)
                fown[call, pl.ds(half * hb, hb), pl.ds(part * sub, sub)] = total.astype(BF16)

    def forward_sum(call):
        qp[call] = qacc[...].reshape(n_plane, OWN, samples)

        def send(k, c):
            p, _, _, dev = plane_dev(k)
            remote(
                qp.at[call, p], qr.at[call, me], q_sem.at[call, 0], q_sem.at[call, 1], dev
            ).start()
            return c

        lax.fori_loop(1, n_plane, send, 0)
        qr[call, me] = qp[call, me]
        wait_bytes(qr.at[call, pl.ds(0, n_plane - 1)], q_sem.at[call, 1])
        return jnp.sum(qr[call], axis=0)

    def share_start(call, value):
        vown[call] = value.astype(BF16)
        vb[call, me] = value.astype(BF16)

        def send(k, c):
            dev = plane_dev(k)[3]
            remote(
                vown.at[call], vb.at[call, me], v_sem.at[call, 0], v_sem.at[call, 1], dev
            ).start()
            return c

        lax.fori_loop(1, n_plane, send, 0)

    def spread_field(call):
        @pl.when(cell == 0)
        def _():
            fpad[call, pl.ds(0, REACH)] = jnp.zeros((REACH, s_rows, LANE), BF16)

        @pl.when(cell == n_cell - 1)
        def _():
            fpad[call, pl.ds(REACH + n_blocks, REACH)] = jnp.zeros((REACH, s_rows, LANE), BF16)

        def part(r):
            return fown.at[call, :, pl.ds(pl.multiple_of(r * s_rows, s_rows), s_rows)]

        def send(k, c):
            r = lax.rem(xc + k, n_r)
            remote(
                part(r),
                fpad.at[call, pl.ds(REACH + xc * bpp, bpp)],
                f_sem.at[call, 0],
                f_sem.at[call, 1],
                (r, cell),
            ).start()
            return c

        lax.fori_loop(1, n_r, send, 0)
        low = xc < n_half

        @pl.when(low & (cell > 0))
        def _():
            def send_low(k, c):
                r = lax.rem(xc + k, n_r)
                remote(
                    part(r),
                    fpad.at[call, pl.ds(REACH + n_blocks + xc * bpp, bpp)],
                    f_sem.at[call, 2],
                    f_sem.at[call, 3],
                    (r, cell - 1),
                ).start()
                return c

            lax.fori_loop(0, n_r, send_low, 0)

        @pl.when((xc >= n_r - n_half) & (cell < n_cell - 1))
        def _():
            def send_high(k, c):
                r = lax.rem(xc + k, n_r)
                remote(
                    part(r),
                    fpad.at[call, pl.ds((xc - (n_r - n_half)) * bpp, bpp)],
                    f_sem.at[call, 4],
                    f_sem.at[call, 5],
                    (r, cell + 1),
                ).start()
                return c

            lax.fori_loop(0, n_r, send_high, 0)

        own = pltpu.make_async_copy(
            part(xc), fpad.at[call, pl.ds(REACH + xc * bpp, bpp)], loc_sem.at[2 + bpp + call]
        )
        own.start()
        own.wait()
        body = fpad.at[call, pl.ds(0, (n_r - 1) * bpp)]
        halo = fpad.at[call, pl.ds(0, REACH)]
        wait_bytes(body, f_sem.at[call, 1])

        @pl.when(cell < n_cell - 1)
        def _():
            wait_bytes(halo, f_sem.at[call, 3])

        @pl.when(cell > 0)
        def _():
            wait_bytes(halo, f_sem.at[call, 5])

    def drain_spread(call):
        body = fpad.at[call, pl.ds(0, (n_r - 1) * bpp)]
        wide = fpad.at[call, pl.ds(0, n_blocks)]
        wait_bytes(body, f_sem.at[call, 0])

        @pl.when((xc < n_half) & (cell > 0))
        def _():
            wait_bytes(wide, f_sem.at[call, 2])

        @pl.when((xc >= n_r - n_half) & (cell < n_cell - 1))
        def _():
            wait_bytes(wide, f_sem.at[call, 4])

    def split(matrix):
        high = matrix.astype(BF16)
        return high, (matrix - high.astype(F32)).astype(BF16)

    def prior_apply(call):
        flat = (n_blocks * s_rows, LANE)
        high, low = split(center_ref[...])
        here = fpad[call, pl.ds(REACH, n_blocks)].reshape(flat)
        acc = nn_dot(here, high) + nn_dot(here, low)
        for band in range(bands_ref.shape[0]):
            offset = offsets_ref[band]
            high, low = split(bands_ref[band])
            ahead = fpad[call, pl.ds(REACH + offset, n_blocks)].reshape(flat)
            acc = acc + nn_dot(ahead, high) + nn_dot(ahead, low)
            behind = fpad[call, pl.ds(REACH - offset, n_blocks)].reshape(flat)
            acc = acc + nt_dot(behind, high) + nt_dot(behind, low)
        smooth[call] = acc.reshape(n_blocks, s_rows, LANE)

    row_id = lax.broadcasted_iota(jnp.int32, (s_rows, samples), 0)
    lane_id = lax.broadcasted_iota(jnp.int32, (s_rows, samples), 1)
    own_lane = lane_id == row_id + xc * s_rows

    def to_lanes(column):
        return jnp.sum(jnp.where(own_lane, column, 0.0), axis=0, keepdims=True)

    def to_column(lanes):
        return jnp.sum(jnp.where(own_lane, lanes, 0.0), axis=1, keepdims=True)

    def field_dot(field, image):
        return to_lanes(jnp.sum(jnp.sum(field * image, axis=0), axis=1, keepdims=True))

    def row_dot(a, b):
        return jnp.sum(a * b, axis=0, keepdims=True)

    def total_start(call, first, second):
        gvec[call] = jnp.concatenate(
            [first, second, jnp.zeros((OWN - 2, samples), F32)], axis=0
        )

        def send(k, c):
            dev = plane_dev(k)[3]
            remote(
                gvec.at[call], gplane.at[call, me], gp_sem.at[call, 0], gp_sem.at[call, 1], dev
            ).start()
            return c

        lax.fori_loop(1, n_plane, send, 0)
        gplane[call, me] = gvec[call]

    def total_middle(call):
        wait_bytes(gplane.at[call, pl.ds(0, n_plane - 1)], gp_sem.at[call, 1])
        gsum[call] = jnp.sum(gplane[call], axis=0)

        def send(k, c):
            _, dev = z_dev(k)
            remote(
                gsum.at[call], gz.at[call, z], gz_sem.at[call, 0], gz_sem.at[call, 1], dev
            ).start()
            return c

        lax.fori_loop(1, n_z, send, 0)
        gz[call, z] = gsum[call]

    def total_end(call):
        wait_bytes(gz.at[call, pl.ds(0, n_z - 1)], gz_sem.at[call, 1])
        total = jnp.sum(gz[call], axis=0)
        return total[0:1], total[1:2]

    def nothing():
        pass

    gather_ring(0, False, nothing, nothing)
    for load in loads:
        load.wait()
    shape = (OWN, observed_ref.shape[1])
    pick = lax.broadcasted_iota(jnp.int32, shape, 1) == lax.broadcasted_iota(
        jnp.int32, shape, 0
    ) + OWN * lax.rem(cell, observed_ref.shape[1] // OWN)
    line = pl.ds(lax.div(cell, observed_ref.shape[1] // OWN), 1)
    own_observed = jnp.sum(jnp.where(pick, observed_ref[line, :], 0.0), axis=1, keepdims=True)
    own_batch = jnp.sum(jnp.where(pick, batch_ref[line, :], 0), axis=1, keepdims=True)
    levels = (OWN, variance_ref.shape[1])
    noise_var = jnp.sum(
        jnp.where(lax.broadcasted_iota(jnp.int32, levels, 1) == own_batch, variance_ref[...], 0.0),
        axis=1,
        keepdims=True,
    )
    target = own_observed + jnp.sqrt(noise_var) * noise_ref[...]
    local_h.wait()
    wait_bytes(hbuf.at[:, pl.ds(0, n_plane - 1)], h_sem.at[1])
    qacc[...] = jnp.zeros((rows, samples), F32)

    def relayout(k, c):
        hm[k] = hbuf[k].astype(F32).reshape(rows, bpp * LANE).astype(BF16)
        accumulate(0, k)
        return c

    lax.fori_loop(0, n_z, relayout, 0)

    first = target - forward_sum(0)
    resid[0] = first
    share_start(0, first)
    reduce_ring(0, nothing, nothing)
    spread_field(0)
    prior_apply(0)

    sbf[...] = smooth[0].astype(BF16)

    def smooth_dst():
        return gath.at[1, z, :, pl.ds(pl.multiple_of(xc * s_rows, s_rows), s_rows)]

    def send_smooth(k, c):
        r = lax.rem(xc + k, n_r)
        remote(
            sbf.at[pl.ds(r * bpp, bpp)], smooth_dst(), s_sem.at[0], s_sem.at[1], (r, cell)
        ).start()
        return c

    lax.fori_loop(1, n_r, send_smooth, 0)
    keep = pltpu.make_async_copy(sbf.at[pl.ds(xc * bpp, bpp)], smooth_dst(), loc_sem.at[4 + bpp])
    keep.start()
    keep.wait()
    others = sbf.at[pl.ds(0, (n_r - 1) * bpp)]
    wait_bytes(others, s_sem.at[1])

    def start_first():
        r0 = resid[0]
        energy = field_dot(fpad[0, pl.ds(REACH, n_blocks)].astype(F32), smooth[0])
        total_start(0, row_dot(r0, r0), energy + row_dot(r0 * noise_var, r0))

    gather_ring(1, True, start_first, lambda: total_middle(0))
    applied = forward_sum(1) + noise_var * resid[0]
    norm0, curve0 = total_end(0)
    alpha0 = norm0 / curve0
    second = resid[0] - alpha0 * applied
    resid[1] = second
    share_start(1, second)

    def start_second():
        r1 = resid[1]
        total_start(1, row_dot(r1, r1), jnp.zeros((1, samples), F32))

    reduce_ring(1, start_second, lambda: total_middle(1))
    spread_field(1)
    prior_apply(1)
    norm1, _ = total_end(1)
    beta = norm1 / norm0
    direction = resid[1] + beta * resid[0]
    beta_column = to_column(beta)
    field0 = fpad[0, pl.ds(REACH, n_blocks)].astype(F32)
    field1 = fpad[1, pl.ds(REACH, n_blocks)].astype(F32)
    energy = field_dot(field1 + beta_column * field0, smooth[1] + beta_column * smooth[0])
    total_start(2, energy + row_dot(direction * noise_var, direction), jnp.zeros((1, samples), F32))
    for call in range(2):
        drain(functools.partial(gather_copy, call))
        drain(functools.partial(reduce_copy, call))
        drain_spread(call)
        wait_bytes(qp.at[call, pl.ds(0, n_plane - 1)], q_sem.at[call, 0])
        wait_bytes(vb.at[call, pl.ds(0, n_plane - 1)], v_sem.at[call, 0])
        wait_bytes(gplane.at[call, pl.ds(0, n_plane - 1)], gp_sem.at[call, 0])
        wait_bytes(gz.at[call, pl.ds(0, n_z - 1)], gz_sem.at[call, 0])
    wait_bytes(others, s_sem.at[0])
    wait_bytes(hbuf.at[:, pl.ds(0, n_plane - 1)], h_sem.at[0])
    local_p.wait()
    total_middle(2)
    curve1, _ = total_end(2)
    alpha1 = norm1 / curve1
    weights_ref[...] = alpha0 * resid[0] + alpha1 * direction
    scale0 = to_column(alpha0 + alpha1 * beta)
    scale1 = to_column(alpha1)
    for b in range(n_blocks):
        columns = slice(b * LANE, (b + 1) * LANE)
        post_ref[:, columns] = (
            own_prior[:, columns].astype(F32) + scale0 * smooth[0, b] + scale1 * smooth[1, b]
        )
    wait_bytes(gplane.at[2, pl.ds(0, n_plane - 1)], gp_sem.at[2, 0])
    wait_bytes(gz.at[2, pl.ds(0, n_z - 1)], gz_sem.at[2, 0])


def local(
    n_r,
    n_z,
    n_y,
    n_low,
    footprint,
    prior_draws,
    observed,
    obs_noise,
    batch_of,
    batch_variance,
    band_offsets,
    center_block,
    band_blocks,
):
    samples = obs_noise.shape[1]
    n_blocks = prior_draws.shape[1] // LANE
    bpp = n_blocks // n_r
    n_plane = n_r * n_y * n_low
    s_rows = samples // n_r
    width = bpp * LANE
    rows = n_plane * OWN
    hb = bpp // 2
    steps = n_z // 2
    tiles = footprint.reshape(OWN, n_z, n_y * n_low, n_r, width).transpose(1, 2, 3, 0, 4)
    count = observed.shape[0]
    lines = (max(count // LANE, 1), min(count, LANE))
    observed = observed.reshape(lines)
    batch_of = batch_of.reshape(lines)
    batch_variance = batch_variance.reshape(1, batch_variance.shape[0])
    vmem = pl.BlockSpec(memory_space=pltpu.VMEM)
    hbm = pl.BlockSpec(memory_space=pl.ANY)
    dma = pltpu.SemaphoreType.DMA
    return pl.pallas_call(
        functools.partial(kernel, (n_r, n_z, n_y, n_low, bpp, samples)),
        out_shape=(
            jax.ShapeDtypeStruct((s_rows, n_blocks * LANE), F32),
            jax.ShapeDtypeStruct((OWN, samples), F32),
        ),
        in_specs=[hbm] * 6 + [pl.BlockSpec(memory_space=pltpu.SMEM), hbm, hbm],
        out_specs=(vmem, vmem),
        scratch_shapes=[
            pltpu.VMEM((n_z, n_plane, OWN, width), BF16),
            pltpu.VMEM((n_z, rows, width), BF16),
            pltpu.VMEM((2, n_z, bpp, samples, LANE), BF16),
            pltpu.VMEM((s_rows, n_blocks * LANE), BF16),
            pltpu.VMEM((2, n_plane, OWN, samples), F32),
            pltpu.VMEM((2, n_plane, OWN, samples), F32),
            pltpu.VMEM((2, OWN, samples), BF16),
            pltpu.VMEM((2, n_plane, OWN, samples), BF16),
            pltpu.VMEM((n_z, bpp, samples, LANE), F32),
            pltpu.VMEM((2, 4 * SPLIT, steps, hb, samples // SPLIT, LANE), BF16),
            pltpu.VMEM((2, 4 * SPLIT, steps, hb, samples // SPLIT, LANE), BF16),
            pltpu.VMEM((2, bpp, samples, LANE), BF16),
            pltpu.VMEM((2, n_blocks + 2 * REACH, s_rows, LANE), BF16),
            pltpu.VMEM((2, n_blocks, s_rows, LANE), F32),
            pltpu.VMEM((n_blocks, s_rows, LANE), BF16),
            pltpu.VMEM((2, OWN, samples), F32),
            pltpu.VMEM((3, OWN, samples), F32),
            pltpu.VMEM((3, n_plane, OWN, samples), F32),
            pltpu.VMEM((3, OWN, samples), F32),
            pltpu.VMEM((3, n_z, OWN, samples), F32),
            pltpu.VMEM((rows, samples), F32),
            pltpu.VMEM(observed.shape, F32),
            pltpu.VMEM((OWN, samples), F32),
            pltpu.VMEM(batch_of.shape, jnp.int32),
            pltpu.VMEM(batch_variance.shape, F32),
            pltpu.VMEM(center_block.shape, F32),
            pltpu.VMEM(band_blocks.shape, F32),
            dma((2,)),
            dma((2, 2)),
            dma((2, 2)),
            dma((4, 2, 4 * SPLIT, steps)),
            dma((2, 6)),
            dma((2,)),
            dma((3, 2)),
            dma((3, 2)),
            dma((11 + bpp,)),
        ],
        compiler_params=pltpu.CompilerParams(
            collective_id=0, has_side_effects=True, vmem_limit_bytes=56 * 1024 * 1024
        ),
    )(
        tiles,
        prior_draws,
        observed,
        obs_noise,
        batch_of,
        batch_variance,
        band_offsets,
        center_block,
        band_blocks,
    )


def solution(mesh, n_y=4):
    n_r = mesh.shape["rcpt"]
    n_z = mesh.shape["cell"] // (n_y * LOW)
    return jax.shard_map(
        functools.partial(local, n_r, n_z, n_y, LOW),
        mesh=mesh,
        in_specs=(
            P(("rcpt", "cell"), None),
            P(None, "cell"),
            P("rcpt"),
            P("rcpt", None),
            P("rcpt"),
            P(),
            P(),
            P(),
            P(),
        ),
        out_specs=(P("rcpt", "cell"), P(("rcpt", "cell"), None)),
        check_vma=False,
    )
```

```python
import functools

import jax
import jax.numpy as jnp
from jax import lax
from jax.experimental import pallas as pl
from jax.experimental.pallas import tpu as pltpu
from jax.sharding import PartitionSpec as P

REACH = 8
SPLIT = 1
LOW = 2
STRIDE = 13
OWN = 8
LANE = 128
MESH = pl.DeviceIdType.MESH
F32 = jnp.float32
BF16 = jnp.bfloat16


def nt_dot(a, b):
    return lax.dot_general(a, b, (((1,), (1,)), ((), ())), preferred_element_type=F32)


def tn_dot(a, b):
    return lax.dot_general(a, b, (((0,), (0,)), ((), ())), preferred_element_type=F32)


def nn_dot(a, b):
    return lax.dot_general(a, b, (((1,), (0,)), ((), ())), preferred_element_type=F32)


def kernel(
    dims,
    h_ref,
    prior_ref,
    observed_hbm,
    noise_hbm,
    batch_hbm,
    variance_hbm,
    offsets_ref,
    center_hbm,
    bands_hbm,
    post_ref,
    weights_ref,
    hbuf,
    hm,
    gath,
    own_prior,
    qp,
    qr,
    vown,
    vb,
    fpart,
    fsend,
    frecv,
    fown,
    fpad,
    smooth,
    sbf,
    resid,
    gvec,
    gplane,
    gsum,
    gz,
    qacc,
    observed_ref,
    noise_ref,
    batch_ref,
    variance_ref,
    center_ref,
    bands_ref,
    h_sem,
    q_sem,
    v_sem,
    ring_sem,
    f_sem,
    s_sem,
    gp_sem,
    gz_sem,
    loc_sem,
):
    n_r, n_z, n_y, n_low, bpp, samples = dims
    n_plane = n_r * n_y * n_low
    n_cell = n_z * n_low * n_y
    n_half = REACH // bpp
    n_blocks = n_r * bpp
    s_rows = samples // n_r
    hb = bpp // 2
    rows = n_plane * OWN
    xc = lax.axis_index("rcpt")
    cell = lax.axis_index("cell")
    near = n_y * n_low
    z = lax.div(cell, near)
    within = lax.rem(cell, near)
    me = xc * near + within

    height = lax.div(cell, n_y)
    level = lax.div(within, n_y)
    kind = lax.rem(xc, 2)

    def paired(xx, low, way):
        away = lax.rem(lax.div(low, n_y) + n_low - level, n_low)
        there = height + away * (1 - 2 * level) * (1 - 2 * way)
        there = lax.rem(there + n_z * n_low, n_z * n_low)
        return (xx, there * n_y + lax.rem(low, n_y))

    def plane_dev(i, way=None):
        p = lax.rem(me + i * STRIDE, n_plane)
        xx, low = lax.div(p, near), lax.rem(p, near)
        return p, xx, low, paired(xx, low, lax.rem(xx, 2) if way is None else way)

    def z_dev(k):
        zz = lax.rem(z + k + n_z, n_z)
        return zz, (xc, zz * near + within)

    def remote(src, dst, send, recv, dev):
        return pltpu.make_async_remote_copy(
            src_ref=src, dst_ref=dst, send_sem=send, recv_sem=recv, device_id=dev, device_id_type=MESH
        )

    def wait_bytes(ref, sem):
        pltpu.make_async_copy(ref, ref, sem).wait()

    local_h = pltpu.make_async_copy(h_ref.at[:, within, xc], hbuf.at[:, me], loc_sem.at[0])
    local_p = pltpu.make_async_copy(
        prior_ref.at[pl.ds(pl.multiple_of(xc * s_rows, s_rows), s_rows), :], own_prior, loc_sem.at[1]
    )
    pieces = []
    for b in range(bpp):
        column = pl.multiple_of((xc * bpp + b) * LANE, LANE)
        piece = pltpu.make_async_copy(
            prior_ref.at[:, pl.ds(column, LANE)], gath.at[0, z, b], loc_sem.at[2 + b]
        )
        piece.start()
        pieces.append(piece)

    barrier = pltpu.get_barrier_semaphore()

    flat = n_r * n_y
    mine = xc * n_y + lax.rem(within, n_y)

    def greet(rise):
        def body(i, c):
            t = lax.rem(mine + i, flat)
            there = lax.rem(height + rise + n_z * n_low, n_z * n_low)
            dev = (lax.div(t, n_y), there * n_y + lax.rem(t, n_y))
            pl.semaphore_signal(barrier, inc=1, device_id=dev, device_id_type=MESH)
            return c

        return body

    lax.fori_loop(1, flat, greet(0), 0)
    lax.fori_loop(0, flat, greet(1), 0)
    lax.fori_loop(0, flat, greet(-1), 0)
    for sign in (1, -1):
        pl.semaphore_signal(barrier, inc=1, device_id=z_dev(sign)[1], device_id_type=MESH)
    pl.semaphore_wait(barrier, 3 * flat - 1 + 2)

    def send_h(i, hop):
        t = lax.rem(mine + i * STRIDE, flat)
        xx = lax.div(t, n_y)
        low = lax.rem(level + hop, n_low) * n_y + lax.rem(t, n_y)
        remote(
            h_ref.at[:, low, xx],
            hbuf.at[:, me],
            h_sem.at[0],
            h_sem.at[1],
            paired(xx, low, lax.rem(xx, 2)),
        ).start()

    def send_same(i, c):
        send_h(i, 0)
        return c

    lax.fori_loop(1, flat, send_same, 0)
    batch = flat * (n_low - 1) // (n_z // 2)

    def send_batch(s):
        def body(i, c):
            send_h(lax.rem(i, flat), 1 + lax.div(i, flat))
            return c

        lax.fori_loop(s * batch, (s + 1) * batch, body, 0)

    local_h.start()
    local_p.start()
    loads = [
        pltpu.make_async_copy(src, dst, loc_sem.at[5 + bpp + i])
        for i, (src, dst) in enumerate(
            (
                (observed_hbm, observed_ref),
                (noise_hbm.at[pl.ds(pl.multiple_of(cell * OWN, OWN), OWN), :], noise_ref),
                (batch_hbm, batch_ref),
                (variance_hbm, variance_ref),
                (center_hbm, center_ref),
                (bands_hbm, bands_ref),
            )
        )
    ]
    for load in loads:
        load.start()
    for piece in pieces:
        piece.wait()

    steps = n_z // 2
    short = n_z - 1 - steps
    middle = max(1, short // 2 + 1)
    sub = samples // SPLIT
    chains = []
    for part in range(SPLIT):
        for half, sign, count in ((0, 1, steps), (0, -1, short), (1, 1, short), (1, -1, steps)):
            chains.append((half, part, sign, count))

    def rotate(k):
        return lax.rem(z + k + n_z, n_z)

    def ring(step_fn, after_step, hook_first, hook_middle):
        for ci, chain in enumerate(chains):
            if chain[3] > 0:
                step_fn(ci, chain, 0, True)
        after_step(0)
        hook_first()

        def body(s, c):
            for ci, chain in enumerate(chains):
                step_fn(ci, chain, s, False)
            after_step(s)
            return c

        lax.fori_loop(1, middle, body, 0)
        hook_middle()
        lax.fori_loop(middle, short, body, 0)
        for s in range(max(short, 1), steps):
            for ci, chain in enumerate(chains):
                if s < chain[3]:
                    step_fn(ci, chain, s, False)
                else:
                    step_fn(ci, chain, s, None)
            after_step(s)

    def drain(copy):
        def body(s, c):
            for ci, chain in enumerate(chains):
                copy(ci, chain, s).wait_send()
            return c

        lax.fori_loop(0, short, body, 0)
        for s in range(short, steps):
            for ci, chain in enumerate(chains):
                if s < chain[3]:
                    copy(ci, chain, s).wait_send()

    def gather_copy(call, ci, chain, s):
        half, part, sign, _ = chain
        origin = rotate(-sign * s)
        piece = gath.at[
            call, origin, pl.ds(half * hb, hb), pl.ds(part * sub, sub)
        ]
        return remote(
            piece, piece, ring_sem.at[call, 0, ci, s], ring_sem.at[call, 1, ci, s], z_dev(sign)[1]
        )

    def accumulate(call, k):
        hz = hm[k]
        for b in range(bpp):
            qacc[...] += nt_dot(hz[:, b * LANE : (b + 1) * LANE], gath[call, k, b])

    def gather_ring(call, multiply, hook_first, hook_middle):
        copy = functools.partial(gather_copy, call)

        def step(ci, chain, s, first):
            if first is not True:
                if s - 1 < chain[3] if isinstance(s, int) else True:
                    copy(ci, chain, s - 1).wait_recv()
            if first is not None:
                copy(ci, chain, s).start()

        def after_step(s):
            if not multiply:
                send_batch(s)
                return
            if isinstance(s, int) and s == 0:
                qacc[...] = jnp.zeros((rows, samples), F32)
                accumulate(call, z)
                return
            accumulate(call, rotate(-s))
            accumulate(call, rotate(s))

        ring(step, after_step, hook_first, hook_middle)
        for ci, chain in enumerate(chains):
            if chain[3] == steps:
                copy(ci, chain, steps - 1).wait_recv()
            elif chain[3] == 0:
                pass
        if multiply:
            accumulate(call, rotate(steps))

    def reduce_copy(call, ci, chain, s):
        return remote(
            fsend.at[call, ci, s],
            frecv.at[call, ci, s],
            ring_sem.at[2 + call, 0, ci, s],
            ring_sem.at[2 + call, 1, ci, s],
            z_dev(chain[2])[1],
        )

    def reduce_ring(call, hook_first, hook_middle):
        copy = functools.partial(reduce_copy, call)
        wait_bytes(vb.at[call, pl.ds(0, n_plane - 1)], v_sem.at[call, 1])
        vector = vb[call].astype(F32).reshape(rows, samples).astype(BF16)

        def project(k):
            product = tn_dot(vector, hm[k])
            for b in range(bpp):
                fpart[k, b] = product[:, b * LANE : (b + 1) * LANE]

        for k in sorted({rotation % n_z for rotation in (steps, steps - 1, 1 - steps)}):
            project(rotate(k))

        def step(ci, chain, s, first):
            half, part, sign, count = chain
            if first is None:
                return
            target = rotate(sign * (count - s))
            value = fpart[target, pl.ds(half * hb, hb), pl.ds(part * sub, sub)]
            if first is not True:
                copy(ci, chain, s - 1).wait_recv()
                value = value + frecv[call, ci, s - 1].astype(F32)
            fsend[call, ci, s] = value.astype(BF16)
            copy(ci, chain, s).start()

        def after_step(s):
            if isinstance(s, int) and steps - 2 - s < 0:
                return
            if isinstance(s, int) and steps - 2 - s == 0:
                project(z)
                return
            project(rotate(steps - 2 - s))
            project(rotate(s + 2 - steps))

        ring(step, after_step, hook_first, hook_middle)
        for ci, chain in enumerate(chains):
            if chain[3] > 0:
                copy(ci, chain, chain[3] - 1).wait_recv()
        for half in range(2):
            for part in range(SPLIT):
                where = (z, pl.ds(half * hb, hb), pl.ds(part * sub, sub))
                total = fpart[where]
                for ci, chain in enumerate(chains):
                    if chain[:2] == (half, part) and chain[3] > 0:
                        total = total + frecv[call, ci, chain[3] - 1].astype(F32)
                fown[call, pl.ds(half * hb, hb), pl.ds(part * sub, sub)] = total.astype(BF16)

    def forward_sum(call):
        qp[call] = qacc[...].reshape(n_plane, OWN, samples)

        def send(k, c):
            p, _, _, dev = plane_dev(k, kind)
            remote(
                qp.at[call, p], qr.at[call, me], q_sem.at[call, 0], q_sem.at[call, 1], dev
            ).start()
            return c

        lax.fori_loop(1, n_plane, send, 0)
        qr[call, me] = qp[call, me]
        wait_bytes(qr.at[call, pl.ds(0, n_plane - 1)], q_sem.at[call, 1])
        return jnp.sum(qr[call], axis=0)

    def share_start(call, value):
        vown[call] = value.astype(BF16)
        vb[call, me] = value.astype(BF16)

        def send(k, c):
            dev = plane_dev(k)[3]
            remote(
                vown.at[call], vb.at[call, me], v_sem.at[call, 0], v_sem.at[call, 1], dev
            ).start()
            return c

        lax.fori_loop(1, n_plane, send, 0)

    def spread_field(call):
        @pl.when(cell == 0)
        def _():
            fpad[call, pl.ds(0, REACH)] = jnp.zeros((REACH, s_rows, LANE), BF16)

        @pl.when(cell == n_cell - 1)
        def _():
            fpad[call, pl.ds(REACH + n_blocks, REACH)] = jnp.zeros((REACH, s_rows, LANE), BF16)

        def part(r):
            return fown.at[call, :, pl.ds(pl.multiple_of(r * s_rows, s_rows), s_rows)]

        def send(k, c):
            r = lax.rem(xc + k, n_r)
            remote(
                part(r),
                fpad.at[call, pl.ds(REACH + xc * bpp, bpp)],
                f_sem.at[call, 0],
                f_sem.at[call, 1],
                (r, cell),
            ).start()
            return c

        lax.fori_loop(1, n_r, send, 0)
        low = xc < n_half

        @pl.when(low & (cell > 0))
        def _():
            def send_low(k, c):
                r = lax.rem(xc + k, n_r)
                remote(
                    part(r),
                    fpad.at[call, pl.ds(REACH + n_blocks + xc * bpp, bpp)],
                    f_sem.at[call, 2],
                    f_sem.at[call, 3],
                    (r, cell - 1),
                ).start()
                return c

            lax.fori_loop(0, n_r, send_low, 0)

        @pl.when((xc >= n_r - n_half) & (cell < n_cell - 1))
        def _():
            def send_high(k, c):
                r = lax.rem(xc + k, n_r)
                remote(
                    part(r),
                    fpad.at[call, pl.ds((xc - (n_r - n_half)) * bpp, bpp)],
                    f_sem.at[call, 4],
                    f_sem.at[call, 5],
                    (r, cell + 1),
                ).start()
                return c

            lax.fori_loop(0, n_r, send_high, 0)

        own = pltpu.make_async_copy(
            part(xc), fpad.at[call, pl.ds(REACH + xc * bpp, bpp)], loc_sem.at[2 + bpp + call]
        )
        own.start()
        own.wait()
        body = fpad.at[call, pl.ds(0, (n_r - 1) * bpp)]
        halo = fpad.at[call, pl.ds(0, REACH)]
        wait_bytes(body, f_sem.at[call, 1])

        @pl.when(cell < n_cell - 1)
        def _():
            wait_bytes(halo, f_sem.at[call, 3])

        @pl.when(cell > 0)
        def _():
            wait_bytes(halo, f_sem.at[call, 5])

    def drain_spread(call):
        body = fpad.at[call, pl.ds(0, (n_r - 1) * bpp)]
        wide = fpad.at[call, pl.ds(0, n_blocks)]
        wait_bytes(body, f_sem.at[call, 0])

        @pl.when((xc < n_half) & (cell > 0))
        def _():
            wait_bytes(wide, f_sem.at[call, 2])

        @pl.when((xc >= n_r - n_half) & (cell < n_cell - 1))
        def _():
            wait_bytes(wide, f_sem.at[call, 4])

    def split(matrix):
        high = matrix.astype(BF16)
        return high, (matrix - high.astype(F32)).astype(BF16)

    def prior_apply(call):
        flat = (n_blocks * s_rows, LANE)
        high, low = split(center_ref[...])
        here = fpad[call, pl.ds(REACH, n_blocks)].reshape(flat)
        acc = nn_dot(here, high) + nn_dot(here, low)
        for band in range(bands_ref.shape[0]):
            offset = offsets_ref[band]
            high, low = split(bands_ref[band])
            ahead = fpad[call, pl.ds(REACH + offset, n_blocks)].reshape(flat)
            acc = acc + nn_dot(ahead, high) + nn_dot(ahead, low)
            behind = fpad[call, pl.ds(REACH - offset, n_blocks)].reshape(flat)
            acc = acc + nt_dot(behind, high) + nt_dot(behind, low)
        smooth[call] = acc.reshape(n_blocks, s_rows, LANE)

    row_id = lax.broadcasted_iota(jnp.int32, (s_rows, samples), 0)
    lane_id = lax.broadcasted_iota(jnp.int32, (s_rows, samples), 1)
    own_lane = lane_id == row_id + xc * s_rows

    def to_lanes(column):
        return jnp.sum(jnp.where(own_lane, column, 0.0), axis=0, keepdims=True)

    def to_column(lanes):
        return jnp.sum(jnp.where(own_lane, lanes, 0.0), axis=1, keepdims=True)

    def field_dot(field, image):
        return to_lanes(jnp.sum(jnp.sum(field * image, axis=0), axis=1, keepdims=True))

    def row_dot(a, b):
        return jnp.sum(a * b, axis=0, keepdims=True)

    def total_start(call, first, second):
        gvec[call] = jnp.concatenate(
            [first, second, jnp.zeros((OWN - 2, samples), F32)], axis=0
        )

        def send(k, c):
            dev = plane_dev(k, 0)[3]
            remote(
                gvec.at[call], gplane.at[call, me], gp_sem.at[call, 0], gp_sem.at[call, 1], dev
            ).start()
            return c

        lax.fori_loop(1, n_plane, send, 0)
        gplane[call, me] = gvec[call]

    def total_middle(call):
        wait_bytes(gplane.at[call, pl.ds(0, n_plane - 1)], gp_sem.at[call, 1])
        gsum[call] = jnp.sum(gplane[call], axis=0)

        def send(k, c):
            _, dev = z_dev(k)
            remote(
                gsum.at[call], gz.at[call, z], gz_sem.at[call, 0], gz_sem.at[call, 1], dev
            ).start()
            return c

        lax.fori_loop(1, n_z, send, 0)
        gz[call, z] = gsum[call]

    def total_end(call):
        wait_bytes(gz.at[call, pl.ds(0, n_z - 1)], gz_sem.at[call, 1])
        total = jnp.sum(gz[call], axis=0)
        return total[0:1], total[1:2]

    def nothing():
        pass

    gather_ring(0, False, nothing, nothing)
    for load in loads:
        load.wait()
    shape = (OWN, observed_ref.shape[1])
    pick = lax.broadcasted_iota(jnp.int32, shape, 1) == lax.broadcasted_iota(
        jnp.int32, shape, 0
    ) + OWN * lax.rem(cell, observed_ref.shape[1] // OWN)
    line = pl.ds(lax.div(cell, observed_ref.shape[1] // OWN), 1)
    own_observed = jnp.sum(jnp.where(pick, observed_ref[line, :], 0.0), axis=1, keepdims=True)
    own_batch = jnp.sum(jnp.where(pick, batch_ref[line, :], 0), axis=1, keepdims=True)
    levels = (OWN, variance_ref.shape[1])
    noise_var = jnp.sum(
        jnp.where(lax.broadcasted_iota(jnp.int32, levels, 1) == own_batch, variance_ref[...], 0.0),
        axis=1,
        keepdims=True,
    )
    target = own_observed + jnp.sqrt(noise_var) * noise_ref[...]
    local_h.wait()
    wait_bytes(hbuf.at[:, pl.ds(0, n_plane - 1)], h_sem.at[1])
    qacc[...] = jnp.zeros((rows, samples), F32)

    def relayout(k, c):
        hm[k] = hbuf[k].astype(F32).reshape(rows, bpp * LANE).astype(BF16)
        accumulate(0, k)
        return c

    lax.fori_loop(0, n_z, relayout, 0)

    first = target - forward_sum(0)
    resid[0] = first
    share_start(0, first)
    reduce_ring(0, nothing, nothing)
    spread_field(0)
    prior_apply(0)

    sbf[...] = smooth[0].astype(BF16)

    def smooth_dst():
        return gath.at[1, z, :, pl.ds(pl.multiple_of(xc * s_rows, s_rows), s_rows)]

    def send_smooth(k, c):
        r = lax.rem(xc + k, n_r)
        remote(
            sbf.at[pl.ds(r * bpp, bpp)], smooth_dst(), s_sem.at[0], s_sem.at[1], (r, cell)
        ).start()
        return c

    lax.fori_loop(1, n_r, send_smooth, 0)
    keep = pltpu.make_async_copy(sbf.at[pl.ds(xc * bpp, bpp)], smooth_dst(), loc_sem.at[4 + bpp])
    keep.start()
    keep.wait()
    others = sbf.at[pl.ds(0, (n_r - 1) * bpp)]
    wait_bytes(others, s_sem.at[1])

    def start_first():
        r0 = resid[0]
        energy = field_dot(fpad[0, pl.ds(REACH, n_blocks)].astype(F32), smooth[0])
        total_start(0, row_dot(r0, r0), energy + row_dot(r0 * noise_var, r0))

    gather_ring(1, True, start_first, lambda: total_middle(0))
    applied = forward_sum(1) + noise_var * resid[0]
    norm0, curve0 = total_end(0)
    alpha0 = norm0 / curve0
    second = resid[0] - alpha0 * applied
    resid[1] = second
    share_start(1, second)

    def start_second():
        r1 = resid[1]
        total_start(1, row_dot(r1, r1), jnp.zeros((1, samples), F32))

    reduce_ring(1, start_second, lambda: total_middle(1))
    spread_field(1)
    prior_apply(1)
    norm1, _ = total_end(1)
    beta = norm1 / norm0
    direction = resid[1] + beta * resid[0]
    beta_column = to_column(beta)
    field0 = fpad[0, pl.ds(REACH, n_blocks)].astype(F32)
    field1 = fpad[1, pl.ds(REACH, n_blocks)].astype(F32)
    energy = field_dot(field1 + beta_column * field0, smooth[1] + beta_column * smooth[0])
    total_start(2, energy + row_dot(direction * noise_var, direction), jnp.zeros((1, samples), F32))
    for call in range(2):
        drain(functools.partial(gather_copy, call))
        drain(functools.partial(reduce_copy, call))
        drain_spread(call)
        wait_bytes(qp.at[call, pl.ds(0, n_plane - 1)], q_sem.at[call, 0])
        wait_bytes(vb.at[call, pl.ds(0, n_plane - 1)], v_sem.at[call, 0])
        wait_bytes(gplane.at[call, pl.ds(0, n_plane - 1)], gp_sem.at[call, 0])
        wait_bytes(gz.at[call, pl.ds(0, n_z - 1)], gz_sem.at[call, 0])
    wait_bytes(others, s_sem.at[0])
    wait_bytes(hbuf.at[:, pl.ds(0, n_plane - 1)], h_sem.at[0])
    local_p.wait()
    total_middle(2)
    curve1, _ = total_end(2)
    alpha1 = norm1 / curve1
    weights_ref[...] = alpha0 * resid[0] + alpha1 * direction
    scale0 = to_column(alpha0 + alpha1 * beta)
    scale1 = to_column(alpha1)
    for b in range(n_blocks):
        columns = slice(b * LANE, (b + 1) * LANE)
        post_ref[:, columns] = (
            own_prior[:, columns].astype(F32) + scale0 * smooth[0, b] + scale1 * smooth[1, b]
        )
    wait_bytes(gplane.at[2, pl.ds(0, n_plane - 1)], gp_sem.at[2, 0])
    wait_bytes(gz.at[2, pl.ds(0, n_z - 1)], gz_sem.at[2, 0])


def local(
    n_r,
    n_z,
    n_y,
    n_low,
    footprint,
    prior_draws,
    observed,
    obs_noise,
    batch_of,
    batch_variance,
    band_offsets,
    center_block,
    band_blocks,
):
    samples = obs_noise.shape[1]
    n_blocks = prior_draws.shape[1] // LANE
    bpp = n_blocks // n_r
    n_plane = n_r * n_y * n_low
    s_rows = samples // n_r
    width = bpp * LANE
    rows = n_plane * OWN
    hb = bpp // 2
    steps = n_z // 2
    tiles = footprint.reshape(OWN, n_z, n_y * n_low, n_r, width).transpose(1, 2, 3, 0, 4)
    count = observed.shape[0]
    lines = (max(count // LANE, 1), min(count, LANE))
    observed = observed.reshape(lines)
    batch_of = batch_of.reshape(lines)
    batch_variance = batch_variance.reshape(1, batch_variance.shape[0])
    vmem = pl.BlockSpec(memory_space=pltpu.VMEM)
    hbm = pl.BlockSpec(memory_space=pl.ANY)
    dma = pltpu.SemaphoreType.DMA
    return pl.pallas_call(
        functools.partial(kernel, (n_r, n_z, n_y, n_low, bpp, samples)),
        out_shape=(
            jax.ShapeDtypeStruct((s_rows, n_blocks * LANE), F32),
            jax.ShapeDtypeStruct((OWN, samples), F32),
        ),
        in_specs=[hbm] * 6 + [pl.BlockSpec(memory_space=pltpu.SMEM), hbm, hbm],
        out_specs=(vmem, vmem),
        scratch_shapes=[
            pltpu.VMEM((n_z, n_plane, OWN, width), BF16),
            pltpu.VMEM((n_z, rows, width), BF16),
            pltpu.VMEM((2, n_z, bpp, samples, LANE), BF16),
            pltpu.VMEM((s_rows, n_blocks * LANE), BF16),
            pltpu.VMEM((2, n_plane, OWN, samples), F32),
            pltpu.VMEM((2, n_plane, OWN, samples), F32),
            pltpu.VMEM((2, OWN, samples), BF16),
            pltpu.VMEM((2, n_plane, OWN, samples), BF16),
            pltpu.VMEM((n_z, bpp, samples, LANE), F32),
            pltpu.VMEM((2, 4 * SPLIT, steps, hb, samples // SPLIT, LANE), BF16),
            pltpu.VMEM((2, 4 * SPLIT, steps, hb, samples // SPLIT, LANE), BF16),
            pltpu.VMEM((2, bpp, samples, LANE), BF16),
            pltpu.VMEM((2, n_blocks + 2 * REACH, s_rows, LANE), BF16),
            pltpu.VMEM((2, n_blocks, s_rows, LANE), F32),
            pltpu.VMEM((n_blocks, s_rows, LANE), BF16),
            pltpu.VMEM((2, OWN, samples), F32),
            pltpu.VMEM((3, OWN, samples), F32),
            pltpu.VMEM((3, n_plane, OWN, samples), F32),
            pltpu.VMEM((3, OWN, samples), F32),
            pltpu.VMEM((3, n_z, OWN, samples), F32),
            pltpu.VMEM((rows, samples), F32),
            pltpu.VMEM(observed.shape, F32),
            pltpu.VMEM((OWN, samples), F32),
            pltpu.VMEM(batch_of.shape, jnp.int32),
            pltpu.VMEM(batch_variance.shape, F32),
            pltpu.VMEM(center_block.shape, F32),
            pltpu.VMEM(band_blocks.shape, F32),
            dma((2,)),
            dma((2, 2)),
            dma((2, 2)),
            dma((4, 2, 4 * SPLIT, steps)),
            dma((2, 6)),
            dma((2,)),
            dma((3, 2)),
            dma((3, 2)),
            dma((11 + bpp,)),
        ],
        compiler_params=pltpu.CompilerParams(
            collective_id=0, has_side_effects=True, vmem_limit_bytes=56 * 1024 * 1024
        ),
    )(
        tiles,
        prior_draws,
        observed,
        obs_noise,
        batch_of,
        batch_variance,
        band_offsets,
        center_block,
        band_blocks,
    )


def solution(mesh, n_y=4):
    n_r = mesh.shape["rcpt"]
    n_z = mesh.shape["cell"] // (n_y * LOW)
    return jax.shard_map(
        functools.partial(local, n_r, n_z, n_y, LOW),
        mesh=mesh,
        in_specs=(
            P(("rcpt", "cell"), None),
            P(None, "cell"),
            P("rcpt"),
            P("rcpt", None),
            P("rcpt"),
            P(),
            P(),
            P(),
            P(),
        ),
        out_specs=(P("rcpt", "cell"), P(("rcpt", "cell"), None)),
        check_vma=False,
    )
```

```python
import functools

import jax
import jax.numpy as jnp
from jax import lax
from jax.experimental import pallas as pl
from jax.experimental.pallas import tpu as pltpu
from jax.sharding import PartitionSpec as P

REACH = 8
SPLIT = 1
LOW = 2
STRIDE = 13
OWN = 8
LANE = 128
MESH = pl.DeviceIdType.MESH
F32 = jnp.float32
BF16 = jnp.bfloat16


def nt_dot(a, b):
    return lax.dot_general(a, b, (((1,), (1,)), ((), ())), preferred_element_type=F32)


def tn_dot(a, b):
    return lax.dot_general(a, b, (((0,), (0,)), ((), ())), preferred_element_type=F32)


def nn_dot(a, b):
    return lax.dot_general(a, b, (((1,), (0,)), ((), ())), preferred_element_type=F32)


def kernel(
    dims,
    h_ref,
    prior_ref,
    observed_hbm,
    noise_hbm,
    batch_hbm,
    variance_hbm,
    offsets_ref,
    center_hbm,
    bands_hbm,
    post_ref,
    weights_ref,
    hbuf,
    hm,
    gath,
    own_prior,
    qp,
    qr,
    vown,
    vb,
    fpart,
    fsend,
    frecv,
    fown,
    fpad,
    smooth,
    sbf,
    resid,
    gvec,
    gplane,
    gsum,
    gz,
    qacc,
    observed_ref,
    noise_ref,
    batch_ref,
    variance_ref,
    center_ref,
    bands_ref,
    h_sem,
    q_sem,
    v_sem,
    ring_sem,
    f_sem,
    s_sem,
    gp_sem,
    gz_sem,
    loc_sem,
):
    n_r, n_z, n_y, n_low, bpp, samples = dims
    n_plane = n_r * n_y * n_low
    n_cell = n_z * n_low * n_y
    n_half = REACH // bpp
    n_blocks = n_r * bpp
    s_rows = samples // n_r
    hb = bpp // 2
    rows = n_plane * OWN
    xc = lax.axis_index("rcpt")
    cell = lax.axis_index("cell")
    near = n_y * n_low
    z = lax.div(cell, near)
    within = lax.rem(cell, near)
    me = xc * near + within

    height = lax.div(cell, n_y)
    level = lax.div(within, n_y)
    kind = lax.rem(xc, 2)

    def paired(xx, low, way):
        away = lax.rem(lax.div(low, n_y) + n_low - level, n_low)
        there = height + away * (1 - 2 * level) * (1 - 2 * way)
        there = lax.rem(there + n_z * n_low, n_z * n_low)
        return (xx, there * n_y + lax.rem(low, n_y))

    def plane_dev(i, way=None):
        p = lax.rem(me + i * STRIDE, n_plane)
        xx, low = lax.div(p, near), lax.rem(p, near)
        return p, xx, low, paired(xx, low, lax.rem(xx, 2) if way is None else way)

    def z_dev(k):
        zz = lax.rem(z + k + n_z, n_z)
        return zz, (xc, zz * near + within)

    def remote(src, dst, send, recv, dev):
        return pltpu.make_async_remote_copy(
            src_ref=src, dst_ref=dst, send_sem=send, recv_sem=recv, device_id=dev, device_id_type=MESH
        )

    def wait_bytes(ref, sem):
        pltpu.make_async_copy(ref, ref, sem).wait()

    local_h = pltpu.make_async_copy(h_ref.at[:, within, xc], hbuf.at[:, me], loc_sem.at[0])
    local_p = pltpu.make_async_copy(
        prior_ref.at[pl.ds(pl.multiple_of(xc * s_rows, s_rows), s_rows), :], own_prior, loc_sem.at[1]
    )
    pieces = []
    for b in range(bpp):
        column = pl.multiple_of((xc * bpp + b) * LANE, LANE)
        piece = pltpu.make_async_copy(
            prior_ref.at[:, pl.ds(column, LANE)], gath.at[0, z, b], loc_sem.at[2 + b]
        )
        piece.start()
        pieces.append(piece)

    barrier = pltpu.get_barrier_semaphore()

    flat = n_r * n_y
    mine = xc * n_y + lax.rem(within, n_y)

    def greet(rise):
        def body(i, c):
            t = lax.rem(mine + i, flat)
            there = lax.rem(height + rise + n_z * n_low, n_z * n_low)
            dev = (lax.div(t, n_y), there * n_y + lax.rem(t, n_y))
            pl.semaphore_signal(barrier, inc=1, device_id=dev, device_id_type=MESH)
            return c

        return body

    lax.fori_loop(1, flat, greet(0), 0)
    lax.fori_loop(0, flat, greet(1), 0)
    lax.fori_loop(0, flat, greet(-1), 0)
    for sign in (1, -1):
        pl.semaphore_signal(barrier, inc=1, device_id=z_dev(sign)[1], device_id_type=MESH)
    pl.semaphore_wait(barrier, 3 * flat - 1 + 2)

    def send_h(i, hop):
        t = lax.rem(mine + i * STRIDE, flat)
        xx = lax.div(t, n_y)
        low = lax.rem(level + hop, n_low) * n_y + lax.rem(t, n_y)
        remote(
            h_ref.at[:, low, xx],
            hbuf.at[:, me],
            h_sem.at[0],
            h_sem.at[1],
            paired(xx, low, lax.rem(xx, 2)),
        ).start()

    def send_same(i, c):
        send_h(i, 0)
        return c

    lax.fori_loop(1, flat, send_same, 0)
    batch = flat * (n_low - 1) // (n_z // 2)

    def send_batch(first, last):
        def body(i, c):
            send_h(lax.rem(i, flat), 1 + lax.div(i, flat))
            return c

        lax.fori_loop(first * batch, last * batch, body, 0)

    local_h.start()
    local_p.start()
    loads = [
        pltpu.make_async_copy(src, dst, loc_sem.at[5 + bpp + i])
        for i, (src, dst) in enumerate(
            (
                (observed_hbm, observed_ref),
                (noise_hbm.at[pl.ds(pl.multiple_of(cell * OWN, OWN), OWN), :], noise_ref),
                (batch_hbm, batch_ref),
                (variance_hbm, variance_ref),
                (center_hbm, center_ref),
                (bands_hbm, bands_ref),
            )
        )
    ]
    for load in loads:
        load.start()
    for piece in pieces:
        piece.wait()

    steps = n_z // 2
    short = n_z - 1 - steps
    middle = max(1, short // 2 + 1)
    sub = samples // SPLIT
    chains = []
    for part in range(SPLIT):
        for half, sign, count in ((0, 1, steps), (0, -1, short), (1, 1, short), (1, -1, steps)):
            chains.append((half, part, sign, count))

    def rotate(k):
        return lax.rem(z + k + n_z, n_z)

    def ring(step_fn, after_step, hook_first, hook_middle):
        for ci, chain in enumerate(chains):
            if chain[3] > 0:
                step_fn(ci, chain, 0, True)
        after_step(0)
        hook_first()

        def body(s, c):
            for ci, chain in enumerate(chains):
                step_fn(ci, chain, s, False)
            after_step(s)
            return c

        lax.fori_loop(1, middle, body, 0)
        hook_middle()
        lax.fori_loop(middle, short, body, 0)
        for s in range(max(short, 1), steps):
            for ci, chain in enumerate(chains):
                if s < chain[3]:
                    step_fn(ci, chain, s, False)
                else:
                    step_fn(ci, chain, s, None)
            after_step(s)

    def drain(copy):
        def body(s, c):
            for ci, chain in enumerate(chains):
                copy(ci, chain, s).wait_send()
            return c

        lax.fori_loop(0, short, body, 0)
        for s in range(short, steps):
            for ci, chain in enumerate(chains):
                if s < chain[3]:
                    copy(ci, chain, s).wait_send()

    def gather_copy(call, ci, chain, s):
        half, part, sign, _ = chain
        origin = rotate(-sign * s)
        piece = gath.at[
            call, origin, pl.ds(half * hb, hb), pl.ds(part * sub, sub)
        ]
        return remote(
            piece, piece, ring_sem.at[call, 0, ci, s], ring_sem.at[call, 1, ci, s], z_dev(sign)[1]
        )

    def accumulate(call, k):
        hz = hm[k]
        for b in range(bpp):
            qacc[...] += nt_dot(hz[:, b * LANE : (b + 1) * LANE], gath[call, k, b])

    def gather_ring(call, multiply, hook_first, hook_middle):
        copy = functools.partial(gather_copy, call)

        def step(ci, chain, s, first):
            if first is not True:
                if s - 1 < chain[3] if isinstance(s, int) else True:
                    copy(ci, chain, s - 1).wait_recv()
            if first is not None:
                copy(ci, chain, s).start()

        def after_step(s):
            if not multiply:
                if isinstance(s, int) and s == 0:
                    send_batch(0, 2)
                elif not (isinstance(s, int) and s == steps - 1):
                    send_batch(s + 1, s + 2)
                return
            if isinstance(s, int) and s == 0:
                qacc[...] = jnp.zeros((rows, samples), F32)
                accumulate(call, z)
                return
            accumulate(call, rotate(-s))
            accumulate(call, rotate(s))

        ring(step, after_step, hook_first, hook_middle)
        for ci, chain in enumerate(chains):
            if chain[3] == steps:
                copy(ci, chain, steps - 1).wait_recv()
            elif chain[3] == 0:
                pass
        if multiply:
            accumulate(call, rotate(steps))

    def reduce_copy(call, ci, chain, s):
        return remote(
            fsend.at[call, ci, s],
            frecv.at[call, ci, s],
            ring_sem.at[2 + call, 0, ci, s],
            ring_sem.at[2 + call, 1, ci, s],
            z_dev(chain[2])[1],
        )

    def reduce_ring(call, hook_first, hook_middle):
        copy = functools.partial(reduce_copy, call)
        wait_bytes(vb.at[call, pl.ds(0, n_plane - 1)], v_sem.at[call, 1])
        vector = vb[call].astype(F32).reshape(rows, samples).astype(BF16)

        def project(k):
            product = tn_dot(vector, hm[k])
            for b in range(bpp):
                fpart[k, b] = product[:, b * LANE : (b + 1) * LANE]

        for k in sorted({rotation % n_z for rotation in (steps, steps - 1, 1 - steps)}):
            project(rotate(k))

        def step(ci, chain, s, first):
            half, part, sign, count = chain
            if first is None:
                return
            target = rotate(sign * (count - s))
            value = fpart[target, pl.ds(half * hb, hb), pl.ds(part * sub, sub)]
            if first is not True:
                copy(ci, chain, s - 1).wait_recv()
                value = value + frecv[call, ci, s - 1].astype(F32)
            fsend[call, ci, s] = value.astype(BF16)
            copy(ci, chain, s).start()

        def after_step(s):
            if isinstance(s, int) and steps - 2 - s < 0:
                return
            if isinstance(s, int) and steps - 2 - s == 0:
                project(z)
                return
            project(rotate(steps - 2 - s))
            project(rotate(s + 2 - steps))

        ring(step, after_step, hook_first, hook_middle)
        for ci, chain in enumerate(chains):
            if chain[3] > 0:
                copy(ci, chain, chain[3] - 1).wait_recv()
        for half in range(2):
            for part in range(SPLIT):
                where = (z, pl.ds(half * hb, hb), pl.ds(part * sub, sub))
                total = fpart[where]
                for ci, chain in enumerate(chains):
                    if chain[:2] == (half, part) and chain[3] > 0:
                        total = total + frecv[call, ci, chain[3] - 1].astype(F32)
                fown[call, pl.ds(half * hb, hb), pl.ds(part * sub, sub)] = total.astype(BF16)

    def forward_sum(call):
        qp[call] = qacc[...].reshape(n_plane, OWN, samples)

        def send(k, c):
            p, _, _, dev = plane_dev(k, kind)
            remote(
                qp.at[call, p], qr.at[call, me], q_sem.at[call, 0], q_sem.at[call, 1], dev
            ).start()
            return c

        lax.fori_loop(1, n_plane, send, 0)
        qr[call, me] = qp[call, me]
        wait_bytes(qr.at[call, pl.ds(0, n_plane - 1)], q_sem.at[call, 1])
        return jnp.sum(qr[call], axis=0)

    def share_start(call, value):
        vown[call] = value.astype(BF16)
        vb[call, me] = value.astype(BF16)

        def send(k, c):
            dev = plane_dev(k)[3]
            remote(
                vown.at[call], vb.at[call, me], v_sem.at[call, 0], v_sem.at[call, 1], dev
            ).start()
            return c

        lax.fori_loop(1, n_plane, send, 0)

    def spread_field(call):
        @pl.when(cell == 0)
        def _():
            fpad[call, pl.ds(0, REACH)] = jnp.zeros((REACH, s_rows, LANE), BF16)

        @pl.when(cell == n_cell - 1)
        def _():
            fpad[call, pl.ds(REACH + n_blocks, REACH)] = jnp.zeros((REACH, s_rows, LANE), BF16)

        def part(r):
            return fown.at[call, :, pl.ds(pl.multiple_of(r * s_rows, s_rows), s_rows)]

        def send(k, c):
            r = lax.rem(xc + k, n_r)
            remote(
                part(r),
                fpad.at[call, pl.ds(REACH + xc * bpp, bpp)],
                f_sem.at[call, 0],
                f_sem.at[call, 1],
                (r, cell),
            ).start()
            return c

        lax.fori_loop(1, n_r, send, 0)
        low = xc < n_half

        @pl.when(low & (cell > 0))
        def _():
            def send_low(k, c):
                r = lax.rem(xc + k, n_r)
                remote(
                    part(r),
                    fpad.at[call, pl.ds(REACH + n_blocks + xc * bpp, bpp)],
                    f_sem.at[call, 2],
                    f_sem.at[call, 3],
                    (r, cell - 1),
                ).start()
                return c

            lax.fori_loop(0, n_r, send_low, 0)

        @pl.when((xc >= n_r - n_half) & (cell < n_cell - 1))
        def _():
            def send_high(k, c):
                r = lax.rem(xc + k, n_r)
                remote(
                    part(r),
                    fpad.at[call, pl.ds((xc - (n_r - n_half)) * bpp, bpp)],
                    f_sem.at[call, 4],
                    f_sem.at[call, 5],
                    (r, cell + 1),
                ).start()
                return c

            lax.fori_loop(0, n_r, send_high, 0)

        own = pltpu.make_async_copy(
            part(xc), fpad.at[call, pl.ds(REACH + xc * bpp, bpp)], loc_sem.at[2 + bpp + call]
        )
        own.start()
        own.wait()
        body = fpad.at[call, pl.ds(0, (n_r - 1) * bpp)]
        halo = fpad.at[call, pl.ds(0, REACH)]
        wait_bytes(body, f_sem.at[call, 1])

        @pl.when(cell < n_cell - 1)
        def _():
            wait_bytes(halo, f_sem.at[call, 3])

        @pl.when(cell > 0)
        def _():
            wait_bytes(halo, f_sem.at[call, 5])

    def drain_spread(call):
        body = fpad.at[call, pl.ds(0, (n_r - 1) * bpp)]
        wide = fpad.at[call, pl.ds(0, n_blocks)]
        wait_bytes(body, f_sem.at[call, 0])

        @pl.when((xc < n_half) & (cell > 0))
        def _():
            wait_bytes(wide, f_sem.at[call, 2])

        @pl.when((xc >= n_r - n_half) & (cell < n_cell - 1))
        def _():
            wait_bytes(wide, f_sem.at[call, 4])

    def split(matrix):
        high = matrix.astype(BF16)
        return high, (matrix - high.astype(F32)).astype(BF16)

    def prior_apply(call):
        flat = (n_blocks * s_rows, LANE)
        high, low = split(center_ref[...])
        here = fpad[call, pl.ds(REACH, n_blocks)].reshape(flat)
        acc = nn_dot(here, high) + nn_dot(here, low)
        for band in range(bands_ref.shape[0]):
            offset = offsets_ref[band]
            high, low = split(bands_ref[band])
            ahead = fpad[call, pl.ds(REACH + offset, n_blocks)].reshape(flat)
            acc = acc + nn_dot(ahead, high) + nn_dot(ahead, low)
            behind = fpad[call, pl.ds(REACH - offset, n_blocks)].reshape(flat)
            acc = acc + nt_dot(behind, high) + nt_dot(behind, low)
        smooth[call] = acc.reshape(n_blocks, s_rows, LANE)

    row_id = lax.broadcasted_iota(jnp.int32, (s_rows, samples), 0)
    lane_id = lax.broadcasted_iota(jnp.int32, (s_rows, samples), 1)
    own_lane = lane_id == row_id + xc * s_rows

    def to_lanes(column):
        return jnp.sum(jnp.where(own_lane, column, 0.0), axis=0, keepdims=True)

    def to_column(lanes):
        return jnp.sum(jnp.where(own_lane, lanes, 0.0), axis=1, keepdims=True)

    def field_dot(field, image):
        return to_lanes(jnp.sum(jnp.sum(field * image, axis=0), axis=1, keepdims=True))

    def row_dot(a, b):
        return jnp.sum(a * b, axis=0, keepdims=True)

    def total_start(call, first, second):
        gvec[call] = jnp.concatenate(
            [first, second, jnp.zeros((OWN - 2, samples), F32)], axis=0
        )

        def send(k, c):
            dev = plane_dev(k, 0)[3]
            remote(
                gvec.at[call], gplane.at[call, me], gp_sem.at[call, 0], gp_sem.at[call, 1], dev
            ).start()
            return c

        lax.fori_loop(1, n_plane, send, 0)
        gplane[call, me] = gvec[call]

    def total_middle(call):
        wait_bytes(gplane.at[call, pl.ds(0, n_plane - 1)], gp_sem.at[call, 1])
        gsum[call] = jnp.sum(gplane[call], axis=0)

        def send(k, c):
            _, dev = z_dev(k)
            remote(
                gsum.at[call], gz.at[call, z], gz_sem.at[call, 0], gz_sem.at[call, 1], dev
            ).start()
            return c

        lax.fori_loop(1, n_z, send, 0)
        gz[call, z] = gsum[call]

    def total_end(call):
        wait_bytes(gz.at[call, pl.ds(0, n_z - 1)], gz_sem.at[call, 1])
        total = jnp.sum(gz[call], axis=0)
        return total[0:1], total[1:2]

    def nothing():
        pass

    gather_ring(0, False, nothing, nothing)
    for load in loads:
        load.wait()
    shape = (OWN, observed_ref.shape[1])
    pick = lax.broadcasted_iota(jnp.int32, shape, 1) == lax.broadcasted_iota(
        jnp.int32, shape, 0
    ) + OWN * lax.rem(cell, observed_ref.shape[1] // OWN)
    line = pl.ds(lax.div(cell, observed_ref.shape[1] // OWN), 1)
    own_observed = jnp.sum(jnp.where(pick, observed_ref[line, :], 0.0), axis=1, keepdims=True)
    own_batch = jnp.sum(jnp.where(pick, batch_ref[line, :], 0), axis=1, keepdims=True)
    levels = (OWN, variance_ref.shape[1])
    noise_var = jnp.sum(
        jnp.where(lax.broadcasted_iota(jnp.int32, levels, 1) == own_batch, variance_ref[...], 0.0),
        axis=1,
        keepdims=True,
    )
    target = own_observed + jnp.sqrt(noise_var) * noise_ref[...]
    local_h.wait()
    wait_bytes(hbuf.at[:, pl.ds(0, n_plane - 1)], h_sem.at[1])
    qacc[...] = jnp.zeros((rows, samples), F32)

    def relayout(k, c):
        hm[k] = hbuf[k].astype(F32).reshape(rows, bpp * LANE).astype(BF16)
        accumulate(0, k)
        return c

    lax.fori_loop(0, n_z, relayout, 0)

    first = target - forward_sum(0)
    resid[0] = first
    share_start(0, first)
    reduce_ring(0, nothing, nothing)
    spread_field(0)
    prior_apply(0)

    sbf[...] = smooth[0].astype(BF16)

    def smooth_dst():
        return gath.at[1, z, :, pl.ds(pl.multiple_of(xc * s_rows, s_rows), s_rows)]

    def send_smooth(k, c):
        r = lax.rem(xc + k, n_r)
        remote(
            sbf.at[pl.ds(r * bpp, bpp)], smooth_dst(), s_sem.at[0], s_sem.at[1], (r, cell)
        ).start()
        return c

    lax.fori_loop(1, n_r, send_smooth, 0)
    keep = pltpu.make_async_copy(sbf.at[pl.ds(xc * bpp, bpp)], smooth_dst(), loc_sem.at[4 + bpp])
    keep.start()
    keep.wait()
    others = sbf.at[pl.ds(0, (n_r - 1) * bpp)]
    wait_bytes(others, s_sem.at[1])

    def start_first():
        r0 = resid[0]
        energy = field_dot(fpad[0, pl.ds(REACH, n_blocks)].astype(F32), smooth[0])
        total_start(0, row_dot(r0, r0), energy + row_dot(r0 * noise_var, r0))

    gather_ring(1, True, start_first, lambda: total_middle(0))
    applied = forward_sum(1) + noise_var * resid[0]
    norm0, curve0 = total_end(0)
    alpha0 = norm0 / curve0
    second = resid[0] - alpha0 * applied
    resid[1] = second
    share_start(1, second)

    def start_second():
        r1 = resid[1]
        total_start(1, row_dot(r1, r1), jnp.zeros((1, samples), F32))

    reduce_ring(1, start_second, lambda: total_middle(1))
    spread_field(1)
    prior_apply(1)
    norm1, _ = total_end(1)
    beta = norm1 / norm0
    direction = resid[1] + beta * resid[0]
    beta_column = to_column(beta)
    field0 = fpad[0, pl.ds(REACH, n_blocks)].astype(F32)
    field1 = fpad[1, pl.ds(REACH, n_blocks)].astype(F32)
    energy = field_dot(field1 + beta_column * field0, smooth[1] + beta_column * smooth[0])
    total_start(2, energy + row_dot(direction * noise_var, direction), jnp.zeros((1, samples), F32))
    for call in range(2):
        drain(functools.partial(gather_copy, call))
        drain(functools.partial(reduce_copy, call))
        drain_spread(call)
        wait_bytes(qp.at[call, pl.ds(0, n_plane - 1)], q_sem.at[call, 0])
        wait_bytes(vb.at[call, pl.ds(0, n_plane - 1)], v_sem.at[call, 0])
        wait_bytes(gplane.at[call, pl.ds(0, n_plane - 1)], gp_sem.at[call, 0])
        wait_bytes(gz.at[call, pl.ds(0, n_z - 1)], gz_sem.at[call, 0])
    wait_bytes(others, s_sem.at[0])
    wait_bytes(hbuf.at[:, pl.ds(0, n_plane - 1)], h_sem.at[0])
    local_p.wait()
    total_middle(2)
    curve1, _ = total_end(2)
    alpha1 = norm1 / curve1
    weights_ref[...] = alpha0 * resid[0] + alpha1 * direction
    scale0 = to_column(alpha0 + alpha1 * beta)
    scale1 = to_column(alpha1)
    for b in range(n_blocks):
        columns = slice(b * LANE, (b + 1) * LANE)
        post_ref[:, columns] = (
            own_prior[:, columns].astype(F32) + scale0 * smooth[0, b] + scale1 * smooth[1, b]
        )
    wait_bytes(gplane.at[2, pl.ds(0, n_plane - 1)], gp_sem.at[2, 0])
    wait_bytes(gz.at[2, pl.ds(0, n_z - 1)], gz_sem.at[2, 0])


def local(
    n_r,
    n_z,
    n_y,
    n_low,
    footprint,
    prior_draws,
    observed,
    obs_noise,
    batch_of,
    batch_variance,
    band_offsets,
    center_block,
    band_blocks,
):
    samples = obs_noise.shape[1]
    n_blocks = prior_draws.shape[1] // LANE
    bpp = n_blocks // n_r
    n_plane = n_r * n_y * n_low
    s_rows = samples // n_r
    width = bpp * LANE
    rows = n_plane * OWN
    hb = bpp // 2
    steps = n_z // 2
    tiles = footprint.reshape(OWN, n_z, n_y * n_low, n_r, width).transpose(1, 2, 3, 0, 4)
    count = observed.shape[0]
    lines = (max(count // LANE, 1), min(count, LANE))
    observed = observed.reshape(lines)
    batch_of = batch_of.reshape(lines)
    batch_variance = batch_variance.reshape(1, batch_variance.shape[0])
    vmem = pl.BlockSpec(memory_space=pltpu.VMEM)
    hbm = pl.BlockSpec(memory_space=pl.ANY)
    dma = pltpu.SemaphoreType.DMA
    return pl.pallas_call(
        functools.partial(kernel, (n_r, n_z, n_y, n_low, bpp, samples)),
        out_shape=(
            jax.ShapeDtypeStruct((s_rows, n_blocks * LANE), F32),
            jax.ShapeDtypeStruct((OWN, samples), F32),
        ),
        in_specs=[hbm] * 6 + [pl.BlockSpec(memory_space=pltpu.SMEM), hbm, hbm],
        out_specs=(vmem, vmem),
        scratch_shapes=[
            pltpu.VMEM((n_z, n_plane, OWN, width), BF16),
            pltpu.VMEM((n_z, rows, width), BF16),
            pltpu.VMEM((2, n_z, bpp, samples, LANE), BF16),
            pltpu.VMEM((s_rows, n_blocks * LANE), BF16),
            pltpu.VMEM((2, n_plane, OWN, samples), F32),
            pltpu.VMEM((2, n_plane, OWN, samples), F32),
            pltpu.VMEM((2, OWN, samples), BF16),
            pltpu.VMEM((2, n_plane, OWN, samples), BF16),
            pltpu.VMEM((n_z, bpp, samples, LANE), F32),
            pltpu.VMEM((2, 4 * SPLIT, steps, hb, samples // SPLIT, LANE), BF16),
            pltpu.VMEM((2, 4 * SPLIT, steps, hb, samples // SPLIT, LANE), BF16),
            pltpu.VMEM((2, bpp, samples, LANE), BF16),
            pltpu.VMEM((2, n_blocks + 2 * REACH, s_rows, LANE), BF16),
            pltpu.VMEM((2, n_blocks, s_rows, LANE), F32),
            pltpu.VMEM((n_blocks, s_rows, LANE), BF16),
            pltpu.VMEM((2, OWN, samples), F32),
            pltpu.VMEM((3, OWN, samples), F32),
            pltpu.VMEM((3, n_plane, OWN, samples), F32),
            pltpu.VMEM((3, OWN, samples), F32),
            pltpu.VMEM((3, n_z, OWN, samples), F32),
            pltpu.VMEM((rows, samples), F32),
            pltpu.VMEM(observed.shape, F32),
            pltpu.VMEM((OWN, samples), F32),
            pltpu.VMEM(batch_of.shape, jnp.int32),
            pltpu.VMEM(batch_variance.shape, F32),
            pltpu.VMEM(center_block.shape, F32),
            pltpu.VMEM(band_blocks.shape, F32),
            dma((2,)),
            dma((2, 2)),
            dma((2, 2)),
            dma((4, 2, 4 * SPLIT, steps)),
            dma((2, 6)),
            dma((2,)),
            dma((3, 2)),
            dma((3, 2)),
            dma((11 + bpp,)),
        ],
        compiler_params=pltpu.CompilerParams(
            collective_id=0, has_side_effects=True, vmem_limit_bytes=56 * 1024 * 1024
        ),
    )(
        tiles,
        prior_draws,
        observed,
        obs_noise,
        batch_of,
        batch_variance,
        band_offsets,
        center_block,
        band_blocks,
    )


def solution(mesh, n_y=4):
    n_r = mesh.shape["rcpt"]
    n_z = mesh.shape["cell"] // (n_y * LOW)
    return jax.shard_map(
        functools.partial(local, n_r, n_z, n_y, LOW),
        mesh=mesh,
        in_specs=(
            P(("rcpt", "cell"), None),
            P(None, "cell"),
            P("rcpt"),
            P("rcpt", None),
            P("rcpt"),
            P(),
            P(),
            P(),
            P(),
        ),
        out_specs=(P("rcpt", "cell"), P(("rcpt", "cell"), None)),
        check_vma=False,
    )
```
